128 devices in a mesh: req: 16 (over x, y), mlp: 8 (over z, core).
Axes of the slice: x: 4, y: 4, z: 4, core: 2. Of those that a mesh axis runs over, the one named last changes fastest.
Arguments:
- tokens: bfloat16 [4096, 2048], P(('req', 'mlp')), may hold values from -6 to 6
- cached_states: float32 [256, 8, 256, 512], P('req', 'mlp'), may hold values from -12 to 12
- prompt_lengths: int32 [256], P('req'), may hold values from 1 to 4096, as said below
- accepted: int32 [256], P('req'), may hold values from 1 to 16, as said below
- owner_slot: int32 [256], P('req'), may hold values from 0 to 255, as said below
- w_query: bfloat16 [2048, 2048], P(None, 'mlp'), may hold values from -0.125 to 0.125
- w_key: bfloat16 [2048, 2048], P(None, 'mlp'), may hold values from -0.125 to 0.125
- w_value: bfloat16 [2048, 4096], P(None, 'mlp'), may hold values from -0.125 to 0.125
- w_gate_ret: bfloat16 [2048, 4096], P(None, 'mlp'), may hold values from -0.125 to 0.125
- w_out: bfloat16 [4096, 2048], P('mlp'), may hold values from -0.09375 to 0.09375
- w_gate: bfloat16 [2048, 4096], P('req', 'mlp'), may hold values from -0.125 to 0.125
- w_up: bfloat16 [2048, 4096], P('req', 'mlp'), may hold values from -0.125 to 0.125
- w_down: bfloat16 [4096, 2048], P('mlp', 'req'), may hold values from -0.09375 to 0.09375
Outputs:
- mixed: bfloat16 [4096, 2048], P(('req', 'mlp'))
- new_states: float32 [256, 8, 256, 512], P('req', 'mlp')
The draws below stay inside these ranges and needn't reach their ends.
Inputs may be any that keep to these rules, and one draw needn't show every extreme that they name: `prompt_lengths`: request r belongs to tenant k = (4 r) // 256, so the four tenants hold consecutive ranges of 64 requests; its prompt length is drawn evenly from 1 to 4^(k + 3). `accepted`: number of leading drafts of request r that are kept, drawn evenly for each request. A permutation of the requests; for request r on req block i = r // 16, owner_slot[r] = j * 16 + i + c with owner block j and 0 <= c < 1, and each pair (j, c) occurs exactly once within a block.
All inputs are finite; a program needn't handle non-finite values.
Results may differ from the reference program's by a relative error of at most 0.017.
Values may be sent and summed in bfloat16 or wider, within the bound.
No kernel may reach another device: no remote copies, remote signals or barrier semaphores. Data moves between devices by JAX's collectives and lax.ppermute only.
A program may use at most 128 MiB of HBM per device.

```python
import math
import jax
import jax.numpy as jnp
from jax import lax

D = 2048
HEADS = 8
DK = 256
DV = 512
FF = 4096
DRAFT = 16
PER_PEER = 1
REQ_DEV = 16
NREQ = 256
TOKENS = 4096
N_REQ = 16


def draw_owner_slot(key, part):
    sub_keys = jax.random.split(jax.random.fold_in(key, 7), N_REQ)
    shuffled = jax.vmap(lambda one_key: jax.random.permutation(one_key, REQ_DEV))(sub_keys)
    sources = jnp.arange(N_REQ, dtype=jnp.int32)[:, None]
    slots = shuffled // PER_PEER * REQ_DEV + sources * PER_PEER + shuffled % PER_PEER
    return slots.reshape(-1).astype(jnp.int32)


def draw_prompt_lengths(key, part):
    request_ids = jnp.arange(NREQ, dtype=jnp.int32)
    tenant = 4 * request_ids // NREQ
    limit = jnp.left_shift(jnp.ones_like(request_ids), 2 * tenant + 6)
    drawn = jax.random.randint(jax.random.fold_in(key, 11), (NREQ,), 0, 4096, dtype=jnp.int32) % limit + 1
    leading = request_ids == tenant * (NREQ // 4)
    drawn = jnp.where(leading, limit, drawn)
    drawn = jnp.where(request_ids == 1, jnp.ones_like(drawn), drawn)
    return drawn.astype(jnp.int32)


def draw_accepted(key, part):
    request_ids = jnp.arange(NREQ, dtype=jnp.int32)
    drawn = jax.random.randint(jax.random.fold_in(key, 13), (NREQ,), 1, DRAFT + 1, dtype=jnp.int32)
    drawn = jnp.where(request_ids == 0, jnp.full_like(drawn, DRAFT), drawn)
    drawn = jnp.where(request_ids == 2, jnp.ones_like(drawn), drawn)
    return drawn.astype(jnp.int32)


def shard_levels(key, shape, shards, smallest, high):
    factor_of, own = 1.0, jax.random.fold_in(key, 6)
    for position, parts in shards:
        draws = jnp.exp(jax.random.uniform(jax.random.fold_in(own, position), (parts,), jnp.float32, smallest / len(shards), high / len(shards)))
        factor_of = factor_of * jnp.repeat(draws, shape[position] // parts).reshape([-1 if axis == position else 1 for axis in range(len(shape))])
    return factor_of


def gaussian(own_key, extent, spread, most, pieces=(), held_as=jnp.bfloat16):
    values = jax.random.normal(own_key, extent, jnp.float32) * spread
    if len(pieces) > 0:
        values = shard_levels(own_key, extent, pieces, -0.22, 0.18) * values
    return jnp.clip(values, min=-most, max=most).astype(held_as)


def setup_inputs(seed: int = 0) -> dict:
    splits = jax.random.split(jax.random.key(seed), 14)
    tokens = gaussian(splits[0], (TOKENS, D), 1.0, 6.0, ((0, 128),))
    cached_states = gaussian(splits[1], (NREQ, HEADS, DK, DV), 2.0, 12.0, ((0, 16), (1, 8)), jnp.float32)
    prompt_lengths = draw_prompt_lengths(jax.random.fold_in(splits[13], 71), 0)
    accepted = draw_accepted(jax.random.fold_in(splits[13], 71), 0)
    owner_slot = draw_owner_slot(jax.random.fold_in(splits[13], 71), 0)
    w_query = gaussian(splits[5], (D, HEADS * DK), D ** -0.5, 0.125, ((1, 8),))
    w_key = gaussian(splits[6], (D, HEADS * DK), D ** -0.5, 0.125, ((1, 8),))
    w_value = gaussian(splits[7], (D, HEADS * DV), D ** -0.5, 0.125, ((1, 8),))
    w_gate_ret = gaussian(splits[8], (D, HEADS * DV), D ** -0.5, 0.125, ((1, 8),))
    w_out = gaussian(splits[9], (HEADS * DV, D), (HEADS * DV) ** -0.5, 0.09375, ((0, 8),))
    w_gate = gaussian(splits[10], (D, FF), D ** -0.5, 0.125, ((0, 16), (1, 8)))
    w_up = gaussian(splits[11], (D, FF), D ** -0.5, 0.125, ((0, 16), (1, 8)))
    w_down = gaussian(splits[12], (FF, D), FF ** -0.5, 0.09375, ((0, 8), (1, 16)))
    return dict(tokens=tokens, cached_states=cached_states, prompt_lengths=prompt_lengths, accepted=accepted, owner_slot=owner_slot, w_query=w_query, w_key=w_key, w_value=w_value, w_gate_ret=w_gate_ret, w_out=w_out, w_gate=w_gate, w_up=w_up, w_down=w_down)


epsilon = 1e-05

def layer_norm(inputs):
    average = lax.optimization_barrier(jnp.mean(inputs, axis=-1, keepdims=True))
    centred = inputs - average
    variance = lax.optimization_barrier(jnp.mean(centred * centred, axis=-1, keepdims=True))
    return centred * lax.rsqrt(variance + epsilon)

def decays(head_count, first_head):
    head_index = jnp.arange(head_count, dtype=jnp.float32) + first_head
    return 1.0 - jnp.exp2(-5.0 - head_index)

def rotate(inputs, positions):
    half_width = inputs.shape[-1] // 2
    frequencies = jnp.exp(-math.log(10000.0) * jnp.arange(half_width, dtype=jnp.float32) / half_width)
    angles = positions[:, :, None] * frequencies[None, None, :]
    cosine_part = jnp.cos(angles)[:, :, None, :]
    sine_part = jnp.sin(angles)[:, :, None, :]
    front_half = inputs[..., :half_width]
    back_half = inputs[..., half_width:]
    return jnp.concatenate([front_half * cosine_part - back_half * sine_part, front_half * sine_part + back_half * cosine_part], axis=-1)

def retention(queries, key_rows, values, states, accepted, gammas):
    draft_count = queries.shape[1]
    draft_pos = jnp.arange(draft_count, dtype=jnp.float32)
    distance = draft_pos[:, None] - draft_pos[None, :]
    decay_mask = jnp.where(distance[None] >= 0, jnp.power(gammas[:, None, None], jnp.maximum(distance, 0.0)[None]), 0.0)
    scores = jnp.einsum('rthd,rshd->rhts', queries.astype(jnp.float32), key_rows.astype(jnp.float32))
    weights = (scores * decay_mask[None]).astype(jnp.bfloat16)
    within = jnp.einsum('rhts,rshv->rthv', weights.astype(jnp.float32), values.astype(jnp.float32))
    carried = jnp.einsum('rthd,rhdv->rthv', queries.astype(jnp.float32), states, precision=lax.Precision.HIGHEST)
    carried = carried * jnp.power(gammas[None, None, :, None], draft_pos[None, :, None, None] + 1.0)
    outputs = within + carried
    accepted_f = accepted.astype(jnp.float32)
    exponent = accepted_f[:, None, None] - 1.0 - draft_pos[None, None, :]
    draft_weights = jnp.where(exponent >= 0, jnp.power(gammas[None, :, None], jnp.maximum(exponent, 0.0)), 0.0)
    old_part = jnp.power(gammas[None, :], accepted_f[:, None])[:, :, None, None] * states
    scaled = key_rows.astype(jnp.float32) * jnp.transpose(draft_weights, (0, 2, 1))[..., None]
    update = jnp.einsum('rshd,rshv->rhdv', scaled, values.astype(jnp.float32), precision=lax.Precision.HIGHEST)
    return (outputs, old_part + update)

def reference(tokens, cached_states, prompt_lengths, accepted, owner_slot, w_query, w_key, w_value, w_gate_ret, w_out, w_gate, w_up, w_down):
    normed = layer_norm(tokens.astype(jnp.float32)).astype(jnp.bfloat16)
    queries = jnp.dot(normed, w_query, preferred_element_type=jnp.float32).reshape(NREQ, DRAFT, HEADS, DK)
    key_rows = (jnp.dot(normed, w_key, preferred_element_type=jnp.float32) * (1.0 / math.sqrt(DK))).reshape(NREQ, DRAFT, HEADS, DK)
    values = jnp.dot(normed, w_value, preferred_element_type=jnp.float32).astype(jnp.bfloat16).reshape(NREQ, DRAFT, HEADS, DV)
    gate_ret = jnp.dot(normed, w_gate_ret, preferred_element_type=jnp.float32).reshape(NREQ, DRAFT, HEADS, DV)
    positions = (prompt_lengths[:, None] + jnp.arange(DRAFT, dtype=jnp.int32)[None, :]).astype(jnp.float32)
    rotated_q = rotate(queries, positions).astype(jnp.bfloat16)
    rotated_k = rotate(key_rows, positions).astype(jnp.bfloat16)
    gammas = decays(HEADS, 0.0)

    def one_request(item):
        result = retention(item[0][None], item[1][None], item[2][None], item[3][None], item[4][None], gammas)
        return (result[0][0], result[1][0])
    outputs, fresh = lax.map(one_request, (rotated_q, rotated_k, values, cached_states, accepted))
    joined = (layer_norm(outputs) * jax.nn.silu(gate_ret)).astype(jnp.bfloat16).reshape(NREQ * DRAFT, HEADS * DV)
    residual = tokens.astype(jnp.float32) + jnp.dot(joined, w_out, preferred_element_type=jnp.float32)
    hidden_in = layer_norm(residual).astype(jnp.bfloat16)
    gate_sum = jnp.dot(hidden_in, w_gate, preferred_element_type=jnp.float32)
    up_sum = jnp.dot(hidden_in, w_up, preferred_element_type=jnp.float32)
    hidden = (jax.nn.silu(gate_sum) * up_sum).astype(jnp.bfloat16)
    mixed = (residual + jnp.dot(hidden, w_down, preferred_element_type=jnp.float32)).astype(jnp.bfloat16)
    new_states = jnp.zeros_like(cached_states).at[owner_slot].set(fresh)
    return (mixed, new_states)
```

```python
import functools
import math

import jax
import jax.numpy as jnp
from jax import lax
from jax.experimental import pallas as pl
from jax.experimental.pallas import tpu as pltpu
from jax.sharding import PartitionSpec as P

DRAFT = 16
EPS = 1e-05
BF = jnp.bfloat16
F32 = jnp.float32
VM = pl.BlockSpec(memory_space=pltpu.VMEM)
SM = pl.BlockSpec(memory_space=pltpu.SMEM)
ANY = pl.BlockSpec(memory_space=pl.ANY)


def sds(shape, dtype):
    return jax.ShapeDtypeStruct(shape, dtype)


def cost(flops, nbytes):
    return pl.CostEstimate(flops=flops, bytes_accessed=nbytes, transcendentals=0)


def params(mib):
    return pltpu.CompilerParams(vmem_limit_bytes=mib << 20)


def norm(v):
    centred = v - jnp.mean(v, axis=-1, keepdims=True)
    variance = jnp.mean(centred * centred, axis=-1, keepdims=True)
    return centred * lax.rsqrt(variance + EPS)


def norm_kernel(x_ref, o_ref):
    o_ref[...] = norm(x_ref[...].astype(F32)).astype(BF)


def norm_rows(x):
    return pl.pallas_call(
        norm_kernel, out_shape=sds(x.shape, BF), in_specs=[VM], out_specs=VM,
        cost_estimate=cost(x.size * 8, x.size * 4), name="norm_rows",
    )(x)


def pack_kernel(g_ref, u_ref, d_ref, o_ref):
    width = g_ref.shape[1]
    o_ref[:, :width] = g_ref[...]
    o_ref[:, width : 2 * width] = u_ref[...]
    o_ref[:, 2 * width :] = d_ref[...].astype(F32).T.astype(BF)


def pack_weights(g, u, d):
    return pl.pallas_call(
        pack_kernel, out_shape=sds((g.shape[0], 3 * g.shape[1]), BF),
        in_specs=[VM] * 3, out_specs=VM,
        cost_estimate=cost(g.size, g.size * 12), name="pack_weights",
    )(g, u, d)


def pair_kernel(a_ref, b_ref, *o_refs):
    rows = o_refs[0].shape[0]
    for i, o_ref in enumerate(o_refs):
        part = pl.ds(i * rows, rows)
        o_ref[...] = (a_ref[part, :].astype(F32) + b_ref[part, :].astype(F32)).astype(BF)


def pair_sum(a, b, pieces):
    rows = a.shape[0] // pieces
    return pl.pallas_call(
        pair_kernel, out_shape=[sds((rows, a.shape[1]), BF)] * pieces,
        in_specs=[VM] * 2, out_specs=[VM] * pieces,
        cost_estimate=cost(a.size, a.size * 6), name="pair_sum",
    )(a, b)


def residual_kernel(x_ref, a_ref, b_ref, c_ref, d_ref, res_ref, hid_ref):
    total = a_ref[...].astype(F32) + b_ref[...].astype(F32)
    total = total + c_ref[...].astype(F32) + d_ref[...].astype(F32)
    res = x_ref[...].astype(F32) + total
    res_ref[...] = res
    hid_ref[...] = norm(res).astype(BF)


def residual_rows(x, parts):
    return pl.pallas_call(
        residual_kernel, out_shape=[sds(x.shape, F32), sds(x.shape, BF)],
        in_specs=[VM] * 5, out_specs=[VM] * 2,
        cost_estimate=cost(x.size * 12, x.size * 16), name="residual_rows",
    )(x, *parts)


def final_kernel(x_ref, a_ref, b_ref, c_ref, d_ref, o_ref):
    total = a_ref[...].astype(F32) + b_ref[...].astype(F32)
    total = total + c_ref[...].astype(F32) + d_ref[...].astype(F32)
    o_ref[...] = (x_ref[...] + total).astype(BF)


def final_rows(x, parts):
    return pl.pallas_call(
        final_kernel, out_shape=sds(x.shape, BF),
        in_specs=[VM] * 5, out_specs=VM,
        cost_estimate=cost(x.size * 6, x.size * 14), name="final_rows",
    )(x, *parts)


def retention_kernel(
    order, *refs, rows_in, key_width, value_width
):
    xs = refs[:8]
    cos_h, sin_h, mask_h, grow_h, wq_h, wk_h, wv_h, wg_h, wo_h, st_h = refs[8:18]
    same_ref, other_ref, k_ref, v_ref = refs[18:22]
    xbuf, cosb, sinb, maskb, growb, wbuf, wob, stb, proj, keep, joined, sems = refs[22:]
    tile = key_width
    copies = []

    def send(src, dst):
        copy = pltpu.make_async_copy(src, dst, sems.at[len(copies)])
        copy.start()
        copies.append(copy)
        return copy

    c_x = [send(x, xbuf.at[pl.ds(i * rows_in, rows_in), :]) for i, x in enumerate(xs)]
    c_w = [send(wk_h, wbuf.at[0]), send(wq_h, wbuf.at[1])]
    c_small = [send(cos_h, cosb), send(sin_h, sinb), send(mask_h, maskb), send(grow_h, growb)]
    for w in (wv_h, wg_h):
        for j in range(value_width // tile):
            c_w.append(send(w.at[:, pl.ds(j * tile, tile)], wbuf.at[len(c_w)]))
    c_s = [send(st_h.at[order[i]], stb.at[i]) for i in range(16)]
    c_o = send(wo_h, wob)
    for c in c_x:
        c.wait()

    x = xbuf[...]

    def project(j):
        c_w[j].wait()
        return jnp.dot(x, wbuf[j], preferred_element_type=F32)

    half = key_width // 2
    key = project(0) * (1.0 / math.sqrt(key_width))
    for c in c_small:
        c.wait()
    cosv, sinv = cosb[...], sinb[...]

    def rotate(u):
        front, back = u[:, :half], u[:, half:]
        return jnp.concatenate(
            [front * cosv - back * sinv, front * sinv + back * cosv], axis=1
        ).astype(BF)

    rk = rotate(key)
    k_ref[...] = rk
    rq = rotate(project(1))
    scores = lax.dot_general(rq, rk, (((1,), (1,)), ((), ())), preferred_element_type=F32)
    weights = (scores * maskb[...]).astype(BF)
    keep[...] = rq
    for j in range(2):
        val = project(2 + j).astype(BF)
        v_ref[:, j * tile : (j + 1) * tile] = val
        proj[:, j * tile : (j + 1) * tile] = jnp.dot(weights, val, preferred_element_type=F32)
    gates = [project(4), project(5)]
    for c in c_s:
        c.wait()
    for i in range(16):
        part = pl.ds(i * DRAFT, DRAFT)
        carried = jnp.dot(keep[part, :], stb[i].astype(BF), preferred_element_type=F32)
        proj[part, :] += carried * growb[part, :]
    normed = norm(proj[...])
    for j in range(2):
        g = gates[j]
        act = g / (1.0 + jnp.exp(-g))
        joined[:, j * tile : (j + 1) * tile] = (
            normed[:, j * tile : (j + 1) * tile] * act
        ).astype(BF)
    c_o.wait()
    rows = joined.shape[0] // 2
    both = joined[...]
    for j in range(wob.shape[1] // 512):
        cols = pl.ds(j * 512, 512)
        out = jnp.dot(both, wob[:, cols], preferred_element_type=F32).astype(BF)
        same_ref[:, cols] = out[:rows]
        other_ref[:, cols] = out[rows:]


def retention(order, xs, cosv, sinv, mask, grow, wq, wk, wv, wg, wo, states):
    rows_in, width = xs[0].shape
    rows = rows_in * 8
    key_width, value_width = wq.shape[1], wv.shape[1]
    body = functools.partial(
        retention_kernel, rows_in=rows_in, key_width=key_width, value_width=value_width
    )
    tiles = (2 * key_width + 2 * value_width) // key_width
    return pl.pallas_call(
        body,
        out_shape=[
            sds((rows // 2, width), BF), sds((rows // 2, width), BF),
            sds((rows, key_width), BF), sds((rows, value_width), BF),
        ],
        in_specs=[SM] + [ANY] * 18,
        out_specs=[VM] * 4,
        scratch_shapes=[
            pltpu.VMEM((rows, width), BF),
            pltpu.VMEM(cosv.shape, F32), pltpu.VMEM(sinv.shape, F32),
            pltpu.VMEM(mask.shape, F32), pltpu.VMEM(grow.shape, F32),
            pltpu.VMEM((tiles, width, key_width), BF),
            pltpu.VMEM(wo.shape, BF),
            pltpu.VMEM(states.shape, F32),
            pltpu.VMEM((rows, value_width), F32),
            pltpu.VMEM((rows, key_width), BF),
            pltpu.VMEM((rows, value_width), BF),
            pltpu.SemaphoreType.DMA((36,)),
        ],
        compiler_params=params(48),
        cost_estimate=cost(2 * rows * width * 2048, 20 << 20),
        name="retention",
    )(order, *xs, cosv, sinv, mask, grow, wq, wk, wv, wg, wo, states)


def fresh_kernel(src, rel, old, st_ref, k_ref, v_ref, dw_ref, o_ref):
    i = pl.program_id(0)
    scaled = (k_ref[...].astype(F32) * dw_ref[...]).astype(BF)
    update = lax.dot_general(
        scaled, v_ref[...], (((0,), (0,)), ((), ())), preferred_element_type=F32
    )
    o_ref[0] = (old[src[i]] * st_ref[0] + update).astype(BF)


def fresh_states(src, rel, old, states, k, v, dw):
    n, key_width, value_width = states.shape
    return pl.pallas_call(
        fresh_kernel,
        grid_spec=pltpu.PrefetchScalarGridSpec(
            num_scalar_prefetch=3,
            grid=(n,),
            in_specs=[
                pl.BlockSpec((1, key_width, value_width), lambda i, s, r, o: (s[i], 0, 0)),
                pl.BlockSpec((DRAFT, key_width), lambda i, s, r, o: (r[i], 0)),
                pl.BlockSpec((DRAFT, value_width), lambda i, s, r, o: (r[i], 0)),
                pl.BlockSpec((DRAFT, key_width), lambda i, s, r, o: (s[i], 0)),
            ],
            out_specs=pl.BlockSpec((1, key_width, value_width), lambda i, s, r, o: (i, 0, 0)),
        ),
        out_shape=sds(states.shape, BF),
        cost_estimate=cost(2 * states.size * DRAFT, states.size * 6),
        name="fresh_states",
    )(src, rel, old, states, k, v, dw)


def widen_kernel(x_ref, o_ref):
    o_ref[...] = x_ref[...].astype(F32)


def widen(x):
    n = x.shape[0]
    block = (2,) + x.shape[1:]
    return pl.pallas_call(
        widen_kernel, grid=(n // 2,),
        in_specs=[pl.BlockSpec(block, lambda i: (i, 0, 0))],
        out_specs=pl.BlockSpec(block, lambda i: (i, 0, 0)),
        out_shape=sds(x.shape, F32),
        cost_estimate=cost(x.size, x.size * 6), name="widen",
    )(x)


def ffn_kernel(*refs, rows_in):
    xs = refs[:8]
    w_h, same_ref, other_ref, xbuf, wbuf, hid, sems = refs[8:]
    copies = []

    def send(src, dst):
        copy = pltpu.make_async_copy(src, dst, sems.at[len(copies)])
        copy.start()
        copies.append(copy)
        return copy

    c_x = [send(x, xbuf.at[pl.ds(i * rows_in, rows_in), :]) for i, x in enumerate(xs)]
    c_w = []
    for t in (0, 2, 1, 3):
        c_w.append(send(w_h.at[:, pl.ds(t * 256, 256)], wbuf.at[t]))
    c_d = [send(w_h.at[:, pl.ds(1024 + t * 256, 256)], wbuf.at[4 + t]) for t in range(2)]
    for c in c_x:
        c.wait()
    x = xbuf[...]
    for t in range(2):
        c_w[2 * t].wait()
        g = jnp.dot(x, wbuf[t], preferred_element_type=F32)
        c_w[2 * t + 1].wait()
        u = jnp.dot(x, wbuf[2 + t], preferred_element_type=F32)
        hid[t] = (g / (1.0 + jnp.exp(-g)) * u).astype(BF)
    for c in c_d:
        c.wait()
    rows = xbuf.shape[0] // 2
    contract = (((1,), (1,)), ((), ()))
    for j in range(xbuf.shape[1] // 512):
        cols = pl.ds(j * 512, 512)
        out = lax.dot_general(hid[0], wbuf[4, cols, :], contract, preferred_element_type=F32)
        out += lax.dot_general(hid[1], wbuf[5, cols, :], contract, preferred_element_type=F32)
        out = out.astype(BF)
        same_ref[:, cols] = out[:rows]
        other_ref[:, cols] = out[rows:]


def ffn(xs, w):
    rows_in, width = xs[0].shape
    rows = rows_in * 8
    return pl.pallas_call(
        functools.partial(ffn_kernel, rows_in=rows_in),
        out_shape=[sds((rows // 2, width), BF)] * 2,
        in_specs=[ANY] * 9,
        out_specs=[VM] * 2,
        scratch_shapes=[
            pltpu.VMEM((rows, width), BF),
            pltpu.VMEM((6, width, 256), BF),
            pltpu.VMEM((2, rows, 256), BF),
            pltpu.SemaphoreType.DMA((14,)),
        ],
        compiler_params=params(32),
        cost_estimate=cost(2 * rows * width * 1536, 9 << 20),
        name="feed_forward",
    )(*xs, w)


def along(shift):
    return [(z * 2 + c, (z + shift) % 4 * 2 + c) for z in range(4) for c in range(2)]


SWAP = [(m, m ^ 1) for m in range(8)]


def gather_rows(x):
    mine = [x] + [lax.ppermute(x, "mlp", along(s)) for s in (1, 2, 3)]
    return mine + [lax.ppermute(v, "mlp", SWAP) for v in mine]


def reduce_rows(same, other):
    pieces = pair_sum(same, lax.ppermute(other, "mlp", SWAP), 4)
    return [pieces[0]] + [lax.ppermute(pieces[s], "mlp", along(-s)) for s in (1, 2, 3)]


def per_device(
    tokens, cached_states, prompt_lengths, accepted, owner_slot,
    w_query, w_key, w_value, w_gate_ret, w_out, w_gate, w_up, w_down,
):
    requests, _, key_width, value_width = cached_states.shape
    states = cached_states.reshape(requests, key_width, value_width)
    w_all = lax.all_gather(pack_weights(w_gate, w_up, w_down), "req", axis=0, tiled=True)
    xs = gather_rows(norm_rows(tokens))

    mlp = lax.axis_index("mlp")
    z, core = mlp // 2, mlp % 2
    ids = jnp.arange(requests, dtype=jnp.int32)
    block = ids // 2
    order = ((z - block % 4) % 4 * 2 + (core + block // 4) % 2) * 2 + ids % 2
    dest = owner_slot // requests
    src = jnp.sum(jnp.where(dest[None, :] == ids[:, None], ids[None, :], 0), axis=1)
    rel = jnp.sum(jnp.where(order[None, :] == src[:, None], ids[None, :], 0), axis=1)
    lengths = jnp.sum(jnp.where(order[:, None] == ids[None, :], prompt_lengths[None, :], 0), axis=1)

    gamma = 1.0 - jnp.exp2(-5.0 - mlp.astype(F32))
    draft = jnp.arange(DRAFT, dtype=jnp.int32)
    position = (lengths[:, None] + draft[None, :]).astype(F32).reshape(-1)
    half = key_width // 2
    freq = jnp.exp(-math.log(10000.0) * jnp.arange(half, dtype=F32) / half)
    angles = position[:, None] * freq[None, :]
    rows = requests * DRAFT
    row = jnp.arange(rows, dtype=jnp.int32)
    gap = row[:, None] - row[None, :]
    inside = (gap >= 0) & (row[:, None] // DRAFT == row[None, :] // DRAFT)
    mask = jnp.where(inside, jnp.power(gamma, jnp.maximum(gap, 0).astype(F32)), 0.0)
    grow = jnp.power(gamma, (row % DRAFT + 1).astype(F32))[:, None]
    accepted_f = accepted.astype(F32)
    exponent = accepted_f[:, None] - 1.0 - draft.astype(F32)[None, :]
    dw = jnp.where(exponent >= 0, jnp.power(gamma, jnp.maximum(exponent, 0.0)), 0.0)
    dw = jnp.broadcast_to(dw.reshape(-1)[:, None], (rows, key_width))
    old = jnp.power(gamma, accepted_f)

    same, other, k, v = retention(
        order, xs, jnp.cos(angles), jnp.sin(angles), mask,
        jnp.broadcast_to(grow, (rows, value_width)),
        w_query, w_key, w_value, w_gate_ret, w_out, states,
    )
    fresh = fresh_states(src, rel, old, states, k, v, dw)
    landed = lax.all_to_all(fresh, "req", split_axis=0, concat_axis=0, tiled=True)
    res, hidden_in = residual_rows(tokens, reduce_rows(same, other))
    same, other = ffn(gather_rows(hidden_in), w_all)
    mixed = final_rows(res, reduce_rows(same, other))
    return mixed, widen(landed).reshape(cached_states.shape)


def solution(mesh):
    return jax.shard_map(
        per_device,
        mesh=mesh,
        in_specs=(
            P(("req", "mlp"), None),
            P("req", "mlp", None, None),
            P("req"),
            P("req"),
            P("req"),
            P(None, "mlp"),
            P(None, "mlp"),
            P(None, "mlp"),
            P(None, "mlp"),
            P("mlp", None),
            P("req", "mlp"),
            P("req", "mlp"),
            P("mlp", "req"),
        ),
        out_specs=(P(("req", "mlp"), None), P("req", "mlp", None, None)),
        check_vma=False,
    )
```

```python
import functools
import math

import jax
import jax.numpy as jnp
from jax import lax
from jax.experimental import pallas as pl
from jax.experimental.pallas import tpu as pltpu
from jax.sharding import PartitionSpec as P

DRAFT = 16
EPS = 1e-05
BF = jnp.bfloat16
F32 = jnp.float32
VM = pl.BlockSpec(memory_space=pltpu.VMEM)
SM = pl.BlockSpec(memory_space=pltpu.SMEM)
ANY = pl.BlockSpec(memory_space=pl.ANY)
HBM = pl.BlockSpec(memory_space=pltpu.HBM)


def sds(shape, dtype):
    return jax.ShapeDtypeStruct(shape, dtype)


def cost(flops, nbytes):
    return pl.CostEstimate(flops=flops, bytes_accessed=nbytes, transcendentals=0)


def params(mib):
    return pltpu.CompilerParams(vmem_limit_bytes=max(mib, 62) << 20)


def norm(v):
    centred = v - jnp.mean(v, axis=-1, keepdims=True)
    variance = jnp.mean(centred * centred, axis=-1, keepdims=True)
    return centred * lax.rsqrt(variance + EPS)


def staged(body, ins, outs, name, flops=0):
    n, m = len(ins), len(outs)

    def kernel(*refs):
        bufs, sems = refs[n + m : -1], refs[-1]
        copies = [pltpu.make_async_copy(refs[i], bufs[i], sems.at[i]) for i in range(n)]
        for c in copies:
            c.start()
        for c in copies:
            c.wait()
        body(*bufs, *refs[n : n + m])

    size = sum(v.size * v.dtype.itemsize for v in list(ins) + list(outs))
    return pl.pallas_call(
        kernel, out_shape=outs, in_specs=[ANY] * n, out_specs=[VM] * m,
        scratch_shapes=[pltpu.VMEM(v.shape, v.dtype) for v in ins]
        + [pltpu.SemaphoreType.DMA((n,))],
        cost_estimate=cost(flops, size), compiler_params=params(16), name=name,
    )(*ins)


def prepare_body(g_ref, u_ref, d_ref, x_ref, y_ref, a_ref, b_ref, o_ref):
    width = g_ref.shape[1]
    half, rows = width // 2, x_ref.shape[0]
    a_ref[:, :width] = g_ref[...]
    a_ref[:, width:] = u_ref[:, :half]
    b_ref[:, :half] = u_ref[:, half:]
    b_ref[:, half:] = d_ref[...].astype(F32).T.astype(BF)
    mine = norm(x_ref[...].astype(F32)).astype(BF)
    theirs = norm(y_ref[...].astype(F32)).astype(BF)
    for i in range(4):
        o_ref[i, :rows, :] = mine
        o_ref[i, rows:, :] = theirs


def prepare(g, u, d, x, y):
    part = sds((g.shape[0], 3 * g.shape[1] // 2), BF)
    both = sds((4, 2 * x.shape[0], x.shape[1]), BF)
    return staged(prepare_body, (g, u, d, x, y), [part, part, both], "prepare")


def pair_body(a_ref, b_ref, *o_refs):
    rows = o_refs[0].shape[0]
    for i, o_ref in enumerate(o_refs):
        part = pl.ds(i * rows, rows)
        o_ref[...] = (a_ref[part, :].astype(F32) + b_ref[part, :].astype(F32)).astype(BF)


def pair_sum(a, b, pieces):
    piece = sds((a.shape[0] // pieces, a.shape[1]), BF)
    return staged(pair_body, (a, b), [piece] * pieces, "pair_sum")


def total(refs):
    out = refs[0][...].astype(F32)
    for r in refs[1:]:
        out = out + r[...].astype(F32)
    return out


def residual_body(x_ref, a_ref, b_ref, c_ref, d_ref, res_ref, hid_ref):
    res = x_ref[...].astype(F32) + total((a_ref, b_ref, c_ref, d_ref))
    res_ref[...] = res
    hid_ref[...] = norm(res).astype(BF)


def residual_rows(x, parts):
    return staged(residual_body, (x, *parts), [sds(x.shape, F32), sds(x.shape, BF)], "residual_rows")


def final_body(x_ref, a_ref, b_ref, c_ref, d_ref, o_ref):
    o_ref[...] = (x_ref[...] + total((a_ref, b_ref, c_ref, d_ref))).astype(BF)


def final_rows(x, parts):
    return staged(final_body, (x, *parts), [sds(x.shape, BF)], "final_rows")[0]


def block_slot(place, request):
    z, core = request // 4, request // 2 % 2
    block = (place[3] + core) % 2 * 4 + (place[2] - z + 4) % 4
    return block * 2 + request % 2


def retention_kernel(
    place, decay, *refs, rows_in, key_width, value_width
):
    x_h, table_h, wq_h, wk_h, wv_h, wg_h, wo_h, st_h = refs[:8]
    same_ref, other_ref, k_ref, v_ref = refs[8:12]
    xbuf, tableb, wbuf, wob, stb, proj, keep, joined, sems = refs[12:]
    tile = key_width
    requests = stb.shape[0]
    rows = xbuf.shape[0]
    copies = []

    def send(src, dst):
        copy = pltpu.make_async_copy(src, dst, sems.at[len(copies)])
        copy.start()
        copies.append(copy)
        return copy

    c_x = []
    for i in range(4):
        for j in range(2):
            at = (4 * j + (place[2] - i + 4) % 4) * rows_in
            rows_at = pl.ds(pl.multiple_of(at, rows_in), rows_in)
            c_x.append(send(x_h.at[i, pl.ds(j * rows_in, rows_in), :], xbuf.at[rows_at, :]))
    c_w = [send(wk_h, wbuf.at[0])]
    c_t = send(table_h, tableb)
    c_w.append(send(wq_h, wbuf.at[1]))
    for w in (wv_h, wg_h):
        for j in range(value_width // tile):
            c_w.append(send(w.at[:, pl.ds(j * tile, tile)], wbuf.at[len(c_w)]))
    c_s = [send(st_h.at[i], stb.at[block_slot(place, i)]) for i in range(requests)]
    c_o = send(wo_h, wob)
    half = key_width // 2
    row = lax.broadcasted_iota(jnp.int32, (rows, rows), 0)
    col = lax.broadcasted_iota(jnp.int32, (rows, rows), 1)
    gap = row - col
    inside = (gap >= 0) & (row // DRAFT == col // DRAFT)
    mask = jnp.where(inside, jnp.exp(decay[0] * jnp.maximum(gap, 0).astype(F32)), 0.0)
    for c in c_x:
        c.wait()

    x = xbuf[...]

    def project(j):
        c_w[j].wait()
        return jnp.dot(x, wbuf[j], preferred_element_type=F32)

    key = project(0) * (1.0 / math.sqrt(key_width))
    c_t.wait()
    cosv, sinv = tableb[:, :half], tableb[:, half : 2 * half]

    def rotate(u):
        front, back = u[:, :half], u[:, half:]
        return jnp.concatenate(
            [front * cosv - back * sinv, front * sinv + back * cosv], axis=1
        ).astype(BF)

    rk = rotate(key)
    fade = tableb[:, 2 * half : 3 * half]
    k_ref[...] = (rk.astype(F32) * jnp.concatenate([fade, fade], axis=1)).astype(BF)
    rq = rotate(project(1))
    scores = lax.dot_general(rq, rk, (((1,), (1,)), ((), ())), preferred_element_type=F32)
    weights = (scores * mask).astype(BF)
    keep[...] = rq
    for j in range(2):
        val = project(2 + j).astype(BF)
        v_ref[:, j * tile : (j + 1) * tile] = val
        proj[:, j * tile : (j + 1) * tile] = jnp.dot(weights, val, preferred_element_type=F32)
    gates = [project(4), project(5)]
    for c in c_s:
        c.wait()
    for i in range(requests):
        part = pl.ds(i * DRAFT, DRAFT)
        carried = jnp.dot(keep[part, :], stb[i].astype(BF), preferred_element_type=F32)
        grow = tableb[part, 3 * half : 4 * half]
        proj[part, :] += carried * jnp.concatenate([grow] * (value_width // half), axis=1)
    normed = norm(proj[...])
    for j in range(2):
        g = gates[j]
        act = g / (1.0 + jnp.exp(-g))
        joined[:, j * tile : (j + 1) * tile] = (
            normed[:, j * tile : (j + 1) * tile] * act
        ).astype(BF)
    c_o.wait()
    both = joined[...]
    for j in range(wob.shape[1] // 512):
        cols = pl.ds(j * 512, 512)
        out = jnp.dot(both, wob[:, cols], preferred_element_type=F32).astype(BF)
        same_ref[:, cols] = out[: rows // 2]
        other_ref[:, cols] = out[rows // 2 :]


def retention(place, decay, xs, table, wq, wk, wv, wg, wo, states):
    rows_in, width = xs.shape[1] // 2, xs.shape[2]
    rows = rows_in * 8
    key_width, value_width = wq.shape[1], wv.shape[1]
    body = functools.partial(
        retention_kernel, rows_in=rows_in, key_width=key_width, value_width=value_width
    )
    tiles = (2 * key_width + 2 * value_width) // key_width
    return pl.pallas_call(
        body,
        out_shape=[
            sds((rows // 2, width), BF), sds((rows // 2, width), BF),
            sds((rows, key_width), BF), sds((rows, value_width), BF),
        ],
        in_specs=[SM] * 2 + [ANY] * 8,
        out_specs=[VM] * 4,
        scratch_shapes=[
            pltpu.VMEM((rows, width), BF),
            pltpu.VMEM(table.shape, F32),
            pltpu.VMEM((tiles, width, key_width), BF),
            pltpu.VMEM(wo.shape, BF),
            pltpu.VMEM(states.shape, F32),
            pltpu.VMEM((rows, value_width), F32),
            pltpu.VMEM((rows, key_width), BF),
            pltpu.VMEM((rows, value_width), BF),
            pltpu.SemaphoreType.DMA((32,)),
        ],
        compiler_params=params(48),
        cost_estimate=cost(2 * rows * width * 2048, 20 << 20),
        name="retention",
    )(place, decay, xs, table, wq, wk, wv, wg, wo, states)


def fresh_kernel(place, owner, old, st_h, k_h, v_h, o_h, stb, kb, vb, ob, in_sems, out_sems):
    n = stb.shape[0]
    copies = [
        pltpu.make_async_copy(k_h, kb, in_sems.at[n]), pltpu.make_async_copy(v_h, vb, in_sems.at[n + 1])
    ]
    loads = [pltpu.make_async_copy(st_h.at[i], stb.at[i], in_sems.at[i]) for i in range(n)]
    stores = [pltpu.make_async_copy(ob.at[i], o_h.at[owner[i] // n], out_sems.at[i]) for i in range(n)]
    for c in copies + loads:
        c.start()
    for c in copies:
        c.wait()
    keys = kb[...].astype(F32).T
    values = vb[...]
    slot = lax.broadcasted_iota(jnp.int32, keys.shape, 1) // DRAFT
    for i in range(n):
        own = jnp.where(slot == block_slot(place, i), keys, 0.0).astype(BF)
        update = jnp.dot(own, values, preferred_element_type=F32)
        loads[i].wait()
        ob[i] = (old[i] * stb[i] + update).astype(BF)
        stores[i].start()
    for c in stores:
        c.wait()


def fresh_states(place, owner, old, states, k, v):
    n = states.shape[0]
    return pl.pallas_call(
        fresh_kernel,
        in_specs=[SM] * 3 + [ANY] * 3,
        out_specs=ANY,
        out_shape=sds(states.shape, BF),
        scratch_shapes=[
            pltpu.VMEM(states.shape, F32), pltpu.VMEM(k.shape, BF), pltpu.VMEM(v.shape, BF),
            pltpu.VMEM(states.shape, BF),
            pltpu.SemaphoreType.DMA((n + 2,)), pltpu.SemaphoreType.DMA((n,)),
        ],
        compiler_params=params(32),
        cost_estimate=cost(2 * states.size * DRAFT, states.size * 6),
        name="fresh_states",
    )(place, owner, old, states, k, v)


def widen_kernel(x_h, o_h, xb, ob, in_sems, out_sems):
    n = x_h.shape[0]
    loads = [pltpu.make_async_copy(x_h.at[i], xb.at[i], in_sems.at[i]) for i in range(n)]
    stores = [pltpu.make_async_copy(ob.at[i], o_h.at[i], out_sems.at[i]) for i in range(n)]
    for c in loads:
        c.start()
    for i in range(n):
        loads[i].wait()
        ob[i] = xb[i].astype(F32)
        stores[i].start()
    for c in stores:
        c.wait()


def widen(x):
    n = x.shape[0]
    return pl.pallas_call(
        widen_kernel, in_specs=[ANY], out_specs=ANY,
        out_shape=sds(x.shape, F32),
        scratch_shapes=[
            pltpu.VMEM(x.shape, BF), pltpu.VMEM(x.shape, F32),
            pltpu.SemaphoreType.DMA((n,)), pltpu.SemaphoreType.DMA((n,)),
        ],
        compiler_params=params(32),
        cost_estimate=cost(x.size, x.size * 6), name="widen",
    )(x)


def ring_order(me):
    return [me, (me + 3) % 4, (me + 1) % 4, (me + 2) % 4]


def ffn_kernel(place, *refs, rows_in):
    xs = refs[:8]
    w_refs = refs[8:16]
    same_ref, other_ref, xbuf, wa, wb, hid, sems = refs[16:]
    copies = []

    def send(src, dst):
        copy = pltpu.make_async_copy(src, dst, sems.at[len(copies)])
        copy.start()
        copies.append(copy)
        return copy

    c_x = [send(x, xbuf.at[pl.ds(i * rows_in, rows_in), :]) for i, x in enumerate(xs)]
    shard = xbuf.shape[1] // 16
    px, py = ring_order(place[0]), ring_order(place[1])

    def spread(refs, buf, outer, inner):
        out = []
        for i in range(16):
            at = outer[i // 4], inner[i % 4]
            where = (at[0] * 4 + at[1]) if buf is wa else (at[1] * 4 + at[0])
            rows = pl.ds(pl.multiple_of(where * shard, shard), shard)
            out.append(send(refs[i // 4].at[pl.ds(i % 4 * shard, shard), :], buf.at[rows, :]))
        return out

    c_a = spread(w_refs[:4], wa, px, py)
    c_b = spread(w_refs[4:], wb, py, px)
    for c in c_x + c_a:
        c.wait()
    x = xbuf[...]

    def act(g, u):
        return (g / (1.0 + jnp.exp(-g)) * u).astype(BF)

    g0 = jnp.dot(x, wa[:, 0:256], preferred_element_type=F32)
    u0 = jnp.dot(x, wa[:, 512:768], preferred_element_type=F32)
    hid[0] = act(g0, u0)
    g1 = jnp.dot(x, wa[:, 256:512], preferred_element_type=F32)
    for c in c_b:
        c.wait()
    u1 = jnp.dot(x, wb[:, 0:256], preferred_element_type=F32)
    hid[1] = act(g1, u1)
    rows = xbuf.shape[0] // 2
    contract = (((1,), (1,)), ((), ()))
    for j in range(xbuf.shape[1] // 512):
        cols = pl.ds(j * 512, 512)
        out = lax.dot_general(hid[0], wb[cols, 256:512], contract, preferred_element_type=F32)
        out += lax.dot_general(hid[1], wb[cols, 512:768], contract, preferred_element_type=F32)
        out = out.astype(BF)
        same_ref[:, cols] = out[:rows]
        other_ref[:, cols] = out[rows:]


def ffn(place, xs, w):
    rows_in, width = xs[0].shape
    rows = rows_in * 8
    return pl.pallas_call(
        functools.partial(ffn_kernel, rows_in=rows_in),
        out_shape=[sds((rows // 2, width), BF)] * 2,
        in_specs=[SM] + [ANY] * 16,
        out_specs=[VM] * 2,
        scratch_shapes=[
            pltpu.VMEM((rows, width), BF),
            pltpu.VMEM((width, 768), BF),
            pltpu.VMEM((width, 768), BF),
            pltpu.VMEM((2, rows, 256), BF),
            pltpu.SemaphoreType.DMA((40,)),
        ],
        compiler_params=params(32),
        cost_estimate=cost(2 * rows * width * 1536, 9 << 20),
        name="feed_forward",
    )(place, *xs, *w)


def hop(v, axis, shift):
    pairs = [
        (x * 4 + y, (x + shift) % 4 * 4 + y if axis == "x" else x * 4 + (y + shift) % 4)
        for x in range(4)
        for y in range(4)
    ]
    return lax.ppermute(v, "req", pairs)


def ring(v, axis):
    before = hop(v, axis, 1)
    return [v, before, hop(v, axis, -1), hop(before, axis, 1)]


def join_kernel(*refs):
    ins, outs, sems = refs[:8], refs[8:10], refs[10]
    rows = ins[0].shape[0]
    copies = [
        pltpu.make_async_copy(r, outs[i // 4].at[pl.ds(i % 4 * rows, rows), :], sems.at[i])
        for i, r in enumerate(ins)
    ]
    for c in copies:
        c.start()
    for c in copies:
        c.wait()


def join(a, b):
    shape = sds((a[0].shape[0] * 4, a[0].shape[1]), BF)
    return pl.pallas_call(
        join_kernel, out_shape=[shape] * 2, in_specs=[ANY] * 8, out_specs=[VM] * 2,
        scratch_shapes=[pltpu.SemaphoreType.DMA((8,))],
        compiler_params=params(4), cost_estimate=cost(0, 4 << 20), name="join",
    )(*a, *b)


def along(shift):
    return [(z * 2 + c, (z + shift) % 4 * 2 + c) for z in range(4) for c in range(2)]


SWAP = [(m, m ^ 1) for m in range(8)]


def gather_rows(x):
    mine = [x] + [lax.ppermute(x, "mlp", along(s)) for s in (1, 2, 3)]
    return mine + [lax.ppermute(v, "mlp", SWAP) for v in mine]


def pair_rows(same, other):
    return pair_sum(same, lax.ppermute(other, "mlp", SWAP), 4)


def reduce_rows(pieces):
    return [pieces[0]] + [lax.ppermute(pieces[s], "mlp", along(-s)) for s in (1, 2, 3)]


def per_device(
    tokens, cached_states, prompt_lengths, accepted, owner_slot,
    w_query, w_key, w_value, w_gate_ret, w_out, w_gate, w_up, w_down,
):
    requests, _, key_width, value_width = cached_states.shape
    states = cached_states.reshape(requests, key_width, value_width)
    req, mlp = lax.axis_index("req"), lax.axis_index("mlp")
    z, core = mlp // 2, mlp % 2
    place = jnp.stack([req // 4, req % 4, z, core]).astype(jnp.int32)
    gamma = 1.0 - jnp.exp2(-5.0 - mlp.astype(F32))
    decay = jnp.log(gamma)
    old = jnp.exp(decay * accepted.astype(F32))

    swapped = lax.ppermute(tokens, "mlp", SWAP)
    part_a, part_b, normed = prepare(w_gate, w_up, w_down, tokens, swapped)
    xs = lax.all_to_all(
        normed, "mlp", split_axis=0, concat_axis=0, tiled=True,
        axis_index_groups=[[c, 2 + c, 4 + c, 6 + c] for c in range(2)],
    )
    block_a, block_b = join(ring(part_a, "y"), ring(part_b, "x"))
    near = [hop(block_a, "x", 1), hop(block_a, "x", -1), hop(block_b, "y", 1), hop(block_b, "y", -1)]

    ids = jnp.arange(requests, dtype=jnp.int32)
    block = ids // 2
    order = ((z - block % 4) % 4 * 2 + (core + block // 4) % 2) * 2 + ids % 2
    pick = order[:, None] == ids[None, :]
    lengths = jnp.sum(jnp.where(pick, prompt_lengths[None, :], 0), axis=1)
    kept = jnp.sum(jnp.where(pick, accepted[None, :], 0), axis=1)
    rows, half = requests * DRAFT, key_width // 2
    draft = jnp.arange(DRAFT, dtype=jnp.int32)
    position = (lengths[:, None] + draft[None, :]).astype(F32).reshape(-1)
    ahead = (kept[:, None] - 1 - draft[None, :]).astype(F32).reshape(-1)
    freq = jnp.exp(-math.log(10000.0) * jnp.arange(half, dtype=F32) / half)
    angles = position[:, None] * freq[None, :]
    fade = jnp.where(ahead >= 0, jnp.exp(decay * jnp.maximum(ahead, 0.0)), 0.0)
    grow = jnp.exp(decay * (jnp.arange(rows, dtype=jnp.int32) % DRAFT + 1).astype(F32))
    wide = (rows, half)
    table = jnp.concatenate(
        [
            jnp.cos(angles), jnp.sin(angles),
            jnp.broadcast_to(fade[:, None], wide), jnp.broadcast_to(grow[:, None], wide),
        ],
        axis=1,
    )

    spot, _ = lax.optimization_barrier((place, block_a))
    same, other, k, v = retention(
        spot, decay.reshape(1), xs, table, w_query, w_key, w_value, w_gate_ret, w_out, states
    )
    near, (same, other, k, v) = lax.optimization_barrier((near, (same, other, k, v)))
    w_all = [block_a, near[0], near[1], hop(near[0], "x", 1), block_b, near[2], near[3], hop(near[2], "y", 1)]
    sums = reduce_rows(pair_rows(same, other))
    k, sums[1] = lax.optimization_barrier((k, sums[1]))
    fresh = fresh_states(place, owner_slot, old, states, k, v)
    fresh, w_all = lax.optimization_barrier((fresh, w_all))
    landed = lax.all_to_all(fresh, "req", split_axis=0, concat_axis=0, tiled=True)
    res, hidden_in = residual_rows(tokens, sums)
    same, other = ffn(place, gather_rows(hidden_in), w_all)
    mixed = final_rows(res, reduce_rows(pair_rows(same, other)))
    return mixed, widen(landed).reshape(cached_states.shape)


def solution(mesh):
    return jax.shard_map(
        per_device,
        mesh=mesh,
        in_specs=(
            P(("req", "mlp"), None),
            P("req", "mlp", None, None),
            P("req"),
            P("req"),
            P("req"),
            P(None, "mlp"),
            P(None, "mlp"),
            P(None, "mlp"),
            P(None, "mlp"),
            P("mlp", None),
            P("req", "mlp"),
            P("req", "mlp"),
            P("mlp", "req"),
        ),
        out_specs=(P(("req", "mlp"), None), P("req", "mlp", None, None)),
        check_vma=False,
    )
```

```python
import functools
import math

import jax
import jax.numpy as jnp
from jax import lax
from jax.experimental import pallas as pl
from jax.experimental.pallas import tpu as pltpu
from jax.sharding import PartitionSpec as P

DRAFT = 16
EPS = 1e-05
BF = jnp.bfloat16
F32 = jnp.float32
VM = pl.BlockSpec(memory_space=pltpu.VMEM)
SM = pl.BlockSpec(memory_space=pltpu.SMEM)
ANY = pl.BlockSpec(memory_space=pl.ANY)
HBM = pl.BlockSpec(memory_space=pltpu.HBM)


def sds(shape, dtype):
    return jax.ShapeDtypeStruct(shape, dtype)


def cost(flops, nbytes):
    return pl.CostEstimate(flops=flops, bytes_accessed=nbytes, transcendentals=0)


def params(mib):
    return pltpu.CompilerParams(vmem_limit_bytes=mib << 20)


def norm(v):
    centred = v - jnp.mean(v, axis=-1, keepdims=True)
    variance = jnp.mean(centred * centred, axis=-1, keepdims=True)
    return centred * lax.rsqrt(variance + EPS)


def staged(body, ins, outs, name, mib=8):
    n, m = len(ins), len(outs)

    def kernel(*refs):
        bufs, sems = refs[n + m : -1], refs[-1]
        copies = [pltpu.make_async_copy(refs[i], bufs[i], sems.at[i]) for i in range(n)]
        for c in copies:
            c.start()
        for c in copies:
            c.wait()
        body(*bufs, *refs[n : n + m])

    size = sum(v.size * v.dtype.itemsize for v in list(ins) + list(outs))
    return pl.pallas_call(
        kernel, out_shape=outs, in_specs=[ANY] * n, out_specs=[VM] * m,
        scratch_shapes=[pltpu.VMEM(v.shape, v.dtype) for v in ins]
        + [pltpu.SemaphoreType.DMA((n,))],
        cost_estimate=cost(0, size), compiler_params=params(mib), name=name,
    )(*ins)


def prepare_body(g_ref, u_ref, d_ref, x_ref, y_ref, a_ref, b_ref, o_ref):
    width = g_ref.shape[1]
    half, rows = width // 2, x_ref.shape[0]
    a_ref[:, :width] = g_ref[...]
    a_ref[:, width:] = u_ref[:, :half]
    b_ref[:, :half] = u_ref[:, half:]
    b_ref[:, half:] = d_ref[...].astype(F32).T.astype(BF)
    mine = norm(x_ref[...].astype(F32)).astype(BF)
    theirs = norm(y_ref[...].astype(F32)).astype(BF)
    for i in range(4):
        o_ref[i, :rows, :] = mine
        o_ref[i, rows:, :] = theirs


def prepare(g, u, d, x, y):
    part = sds((g.shape[0], 3 * g.shape[1] // 2), BF)
    both = sds((4, 2 * x.shape[0], x.shape[1]), BF)
    return staged(prepare_body, (g, u, d, x, y), [part, part, both], "prepare", 62)


def pair_body(a_ref, b_ref, *o_refs):
    rows = o_refs[0].shape[0]
    for i, o_ref in enumerate(o_refs):
        part = pl.ds(i * rows, rows)
        o_ref[...] = (a_ref[part, :].astype(F32) + b_ref[part, :].astype(F32)).astype(BF)


def pair_sum(a, b, pieces):
    piece = sds((a.shape[0] // pieces, a.shape[1]), BF)
    return staged(pair_body, (a, b), [piece] * pieces, "pair_sum")


def total(refs):
    out = refs[0][...].astype(F32)
    for r in refs[1:]:
        out = out + r[...].astype(F32)
    return out


def residual_body(x_ref, a_ref, b_ref, c_ref, d_ref, res_ref, hid_ref):
    res = x_ref[...].astype(F32) + total((a_ref, b_ref, c_ref, d_ref))
    res_ref[...] = res
    hid_ref[...] = norm(res).astype(BF)


def residual_rows(x, parts):
    return staged(residual_body, (x, *parts), [sds(x.shape, F32), sds(x.shape, BF)], "residual_rows")


def final_body(x_ref, a_ref, b_ref, c_ref, d_ref, o_ref):
    o_ref[...] = (x_ref[...] + total((a_ref, b_ref, c_ref, d_ref))).astype(BF)


def final_rows(x, parts):
    return staged(final_body, (x, *parts), [sds(x.shape, BF)], "final_rows")[0]


def block_slot(place, request):
    z, core = request // 4, request // 2 % 2
    block = (place[3] + core) % 2 * 4 + (place[2] - z + 4) % 4
    return block * 2 + request % 2


def retention_kernel(
    place, decay, *refs, rows_in, key_width, value_width
):
    x_h, table_h, wq_h, wk_h, wv_h, wg_h, wo_h, st_h = refs[:8]
    same_ref, other_ref, k_ref, v_ref = refs[8:12]
    xbuf, tableb, wbuf, wob, stb, proj, keep, joined, sems = refs[12:]
    tile = key_width
    requests = stb.shape[0]
    rows = xbuf.shape[0]
    copies = []

    def send(src, dst):
        copy = pltpu.make_async_copy(src, dst, sems.at[len(copies)])
        copy.start()
        copies.append(copy)
        return copy

    c_x = []
    for i in range(4):
        for j in range(2):
            at = (4 * j + (place[2] - i + 4) % 4) * rows_in
            rows_at = pl.ds(pl.multiple_of(at, rows_in), rows_in)
            c_x.append(send(x_h.at[i, pl.ds(j * rows_in, rows_in), :], xbuf.at[rows_at, :]))
    c_w = [send(wk_h, wbuf.at[0])]
    c_t = send(table_h, tableb)
    c_w.append(send(wq_h, wbuf.at[1]))
    for w in (wv_h, wg_h):
        for j in range(value_width // tile):
            c_w.append(send(w.at[:, pl.ds(j * tile, tile)], wbuf.at[len(c_w)]))
    c_s = [send(st_h.at[i], stb.at[block_slot(place, i)]) for i in range(requests)]
    c_o = send(wo_h, wob)
    half = key_width // 2
    row = lax.broadcasted_iota(jnp.int32, (rows, rows), 0)
    col = lax.broadcasted_iota(jnp.int32, (rows, rows), 1)
    gap = row - col
    inside = (gap >= 0) & (row // DRAFT == col // DRAFT)
    mask = jnp.where(inside, jnp.exp(decay[0] * jnp.maximum(gap, 0).astype(F32)), 0.0)
    for c in c_x:
        c.wait()

    x = xbuf[...]

    def project(j):
        c_w[j].wait()
        return jnp.dot(x, wbuf[j], preferred_element_type=F32)

    key = project(0) * (1.0 / math.sqrt(key_width))
    c_t.wait()
    cosv, sinv = tableb[:, :half], tableb[:, half : 2 * half]

    def rotate(u):
        front, back = u[:, :half], u[:, half:]
        return jnp.concatenate(
            [front * cosv - back * sinv, front * sinv + back * cosv], axis=1
        ).astype(BF)

    rk = rotate(key)
    fade = tableb[:, 2 * half : 3 * half]
    k_ref[...] = (rk.astype(F32) * jnp.concatenate([fade, fade], axis=1)).astype(BF)
    rq = rotate(project(1))
    scores = lax.dot_general(rq, rk, (((1,), (1,)), ((), ())), preferred_element_type=F32)
    weights = (scores * mask).astype(BF)
    keep[...] = rq
    for j in range(2):
        val = project(2 + j).astype(BF)
        v_ref[:, j * tile : (j + 1) * tile] = val
        proj[:, j * tile : (j + 1) * tile] = jnp.dot(weights, val, preferred_element_type=F32)
    gates = [project(4), project(5)]
    for c in c_s:
        c.wait()
    for i in range(requests):
        part = pl.ds(i * DRAFT, DRAFT)
        carried = jnp.dot(keep[part, :], stb[i].astype(BF), preferred_element_type=F32)
        grow = tableb[part, 3 * half : 4 * half]
        proj[part, :] += carried * jnp.concatenate([grow] * (value_width // half), axis=1)
    normed = norm(proj[...])
    for j in range(2):
        g = gates[j]
        act = g / (1.0 + jnp.exp(-g))
        joined[:, j * tile : (j + 1) * tile] = (
            normed[:, j * tile : (j + 1) * tile] * act
        ).astype(BF)
    c_o.wait()
    both = joined[...]
    for j in range(wob.shape[1] // 512):
        cols = pl.ds(j * 512, 512)
        out = jnp.dot(both, wob[:, cols], preferred_element_type=F32).astype(BF)
        same_ref[:, cols] = out[: rows // 2]
        other_ref[:, cols] = out[rows // 2 :]


def retention(place, decay, xs, table, wq, wk, wv, wg, wo, states):
    rows_in, width = xs.shape[1] // 2, xs.shape[2]
    rows = rows_in * 8
    key_width, value_width = wq.shape[1], wv.shape[1]
    body = functools.partial(
        retention_kernel, rows_in=rows_in, key_width=key_width, value_width=value_width
    )
    tiles = (2 * key_width + 2 * value_width) // key_width
    return pl.pallas_call(
        body,
        out_shape=[
            sds((rows // 2, width), BF), sds((rows // 2, width), BF),
            sds((rows, key_width), BF), sds((rows, value_width), BF),
        ],
        in_specs=[SM] * 2 + [ANY] * 8,
        out_specs=[VM] * 4,
        scratch_shapes=[
            pltpu.VMEM((rows, width), BF),
            pltpu.VMEM(table.shape, F32),
            pltpu.VMEM((tiles, width, key_width), BF),
            pltpu.VMEM(wo.shape, BF),
            pltpu.VMEM(states.shape, F32),
            pltpu.VMEM((rows, value_width), F32),
            pltpu.VMEM((rows, key_width), BF),
            pltpu.VMEM((rows, value_width), BF),
            pltpu.SemaphoreType.DMA((32,)),
        ],
        compiler_params=params(62),
        cost_estimate=cost(2 * rows * width * 2048, 20 << 20),
        name="retention",
    )(place, decay, xs, table, wq, wk, wv, wg, wo, states)


def fresh_kernel(place, owner, old, st_h, k_h, v_h, o_h, stb, kb, vb, ob, in_sems, out_sems):
    n = stb.shape[0]
    copies = [
        pltpu.make_async_copy(k_h, kb, in_sems.at[n]), pltpu.make_async_copy(v_h, vb, in_sems.at[n + 1])
    ]
    loads = [pltpu.make_async_copy(st_h.at[i], stb.at[i], in_sems.at[i]) for i in range(n)]
    stores = [pltpu.make_async_copy(ob.at[i], o_h.at[owner[i] // n], out_sems.at[i]) for i in range(n)]
    for c in copies + loads:
        c.start()
    for c in copies:
        c.wait()
    keys = kb[...].astype(F32).T
    values = vb[...]
    slot = lax.broadcasted_iota(jnp.int32, keys.shape, 1) // DRAFT
    for i in range(n):
        own = jnp.where(slot == block_slot(place, i), keys, 0.0).astype(BF)
        update = jnp.dot(own, values, preferred_element_type=F32)
        loads[i].wait()
        ob[i] = (old[i] * stb[i] + update).astype(BF)
        stores[i].start()
    for c in stores:
        c.wait()


def fresh_states(place, owner, old, states, k, v):
    n = states.shape[0]
    return pl.pallas_call(
        fresh_kernel,
        in_specs=[SM] * 3 + [ANY] * 3,
        out_specs=ANY,
        out_shape=sds(states.shape, BF),
        scratch_shapes=[
            pltpu.VMEM(states.shape, F32), pltpu.VMEM(k.shape, BF), pltpu.VMEM(v.shape, BF),
            pltpu.VMEM(states.shape, BF),
            pltpu.SemaphoreType.DMA((n + 2,)), pltpu.SemaphoreType.DMA((n,)),
        ],
        compiler_params=params(62),
        cost_estimate=cost(2 * states.size * DRAFT, states.size * 6),
        name="fresh_states",
    )(place, owner, old, states, k, v)


def widen_kernel(x_h, o_h, xb, ob, in_sems, out_sems):
    n = x_h.shape[0]
    loads = [pltpu.make_async_copy(x_h.at[i], xb.at[i], in_sems.at[i]) for i in range(n)]
    stores = [pltpu.make_async_copy(ob.at[i], o_h.at[i], out_sems.at[i]) for i in range(n)]
    for c in loads:
        c.start()
    for i in range(n):
        loads[i].wait()
        ob[i] = xb[i].astype(F32)
        stores[i].start()
    for c in stores:
        c.wait()


def widen(x):
    n = x.shape[0]
    return pl.pallas_call(
        widen_kernel, in_specs=[ANY], out_specs=ANY,
        out_shape=sds(x.shape, F32),
        scratch_shapes=[
            pltpu.VMEM(x.shape, BF), pltpu.VMEM(x.shape, F32),
            pltpu.SemaphoreType.DMA((n,)), pltpu.SemaphoreType.DMA((n,)),
        ],
        compiler_params=params(62),
        cost_estimate=cost(x.size, x.size * 6), name="widen",
    )(x)


def ring_order(me):
    return [me, (me + 3) % 4, (me + 1) % 4, (me + 2) % 4]


def ffn_kernel(place, *refs, rows_in):
    xs = refs[:8]
    w_refs = refs[8:16]
    same_ref, other_ref, xbuf, wa, wb, hid, sems = refs[16:]
    copies = []

    def send(src, dst):
        copy = pltpu.make_async_copy(src, dst, sems.at[len(copies)])
        copy.start()
        copies.append(copy)
        return copy

    c_x = [send(x, xbuf.at[pl.ds(i * rows_in, rows_in), :]) for i, x in enumerate(xs)]
    shard = xbuf.shape[1] // 16
    px, py = ring_order(place[0]), ring_order(place[1])

    def spread(refs, buf, outer, inner):
        out = []
        for i in range(16):
            at = outer[i // 4], inner[i % 4]
            where = (at[0] * 4 + at[1]) if buf is wa else (at[1] * 4 + at[0])
            rows = pl.ds(pl.multiple_of(where * shard, shard), shard)
            out.append(send(refs[i // 4].at[pl.ds(i % 4 * shard, shard), :], buf.at[rows, :]))
        return out

    c_a = spread(w_refs[:4], wa, px, py)
    c_b = spread(w_refs[4:], wb, py, px)
    for c in c_x + c_a:
        c.wait()
    x = xbuf[...]

    def act(g, u):
        return (g / (1.0 + jnp.exp(-g)) * u).astype(BF)

    g0 = jnp.dot(x, wa[:, 0:256], preferred_element_type=F32)
    u0 = jnp.dot(x, wa[:, 512:768], preferred_element_type=F32)
    hid[0] = act(g0, u0)
    g1 = jnp.dot(x, wa[:, 256:512], preferred_element_type=F32)
    for c in c_b:
        c.wait()
    u1 = jnp.dot(x, wb[:, 0:256], preferred_element_type=F32)
    hid[1] = act(g1, u1)
    rows = xbuf.shape[0] // 2
    contract = (((1,), (1,)), ((), ()))
    for j in range(xbuf.shape[1] // 512):
        cols = pl.ds(j * 512, 512)
        out = lax.dot_general(hid[0], wb[cols, 256:512], contract, preferred_element_type=F32)
        out += lax.dot_general(hid[1], wb[cols, 512:768], contract, preferred_element_type=F32)
        out = out.astype(BF)
        same_ref[:, cols] = out[:rows]
        other_ref[:, cols] = out[rows:]


def ffn(place, xs, w):
    rows_in, width = xs[0].shape
    rows = rows_in * 8
    return pl.pallas_call(
        functools.partial(ffn_kernel, rows_in=rows_in),
        out_shape=[sds((rows // 2, width), BF)] * 2,
        in_specs=[SM] + [ANY] * 16,
        out_specs=[VM] * 2,
        scratch_shapes=[
            pltpu.VMEM((rows, width), BF),
            pltpu.VMEM((width, 768), BF),
            pltpu.VMEM((width, 768), BF),
            pltpu.VMEM((2, rows, 256), BF),
            pltpu.SemaphoreType.DMA((40,)),
        ],
        compiler_params=params(62),
        cost_estimate=cost(2 * rows * width * 1536, 9 << 20),
        name="feed_forward",
    )(place, *xs, *w)


def hop(v, axis, shift):
    pairs = [
        (x * 4 + y, (x + shift) % 4 * 4 + y if axis == "x" else x * 4 + (y + shift) % 4)
        for x in range(4)
        for y in range(4)
    ]
    return lax.ppermute(v, "req", pairs)


def ring(v, axis):
    before = hop(v, axis, 1)
    return [v, before, hop(v, axis, -1), hop(before, axis, 1)]


def join_kernel(*refs):
    ins, outs, sems = refs[:8], refs[8:10], refs[10]
    rows = ins[0].shape[0]
    copies = [
        pltpu.make_async_copy(r, outs[i // 4].at[pl.ds(i % 4 * rows, rows), :], sems.at[i])
        for i, r in enumerate(ins)
    ]
    for c in copies:
        c.start()
    for c in copies:
        c.wait()


def join(a, b):
    shape = sds((a[0].shape[0] * 4, a[0].shape[1]), BF)
    return pl.pallas_call(
        join_kernel, out_shape=[shape] * 2, in_specs=[ANY] * 8, out_specs=[VM] * 2,
        scratch_shapes=[pltpu.SemaphoreType.DMA((8,))],
        compiler_params=params(62), cost_estimate=cost(0, 4 << 20), name="join",
    )(*a, *b)


def along(shift):
    return [(z * 2 + c, (z + shift) % 4 * 2 + c) for z in range(4) for c in range(2)]


SWAP = [(m, m ^ 1) for m in range(8)]


def gather_rows(x):
    mine = [x] + [lax.ppermute(x, "mlp", along(s)) for s in (1, 2, 3)]
    return mine + [lax.ppermute(v, "mlp", SWAP) for v in mine]


def pair_rows(same, other):
    return pair_sum(same, lax.ppermute(other, "mlp", SWAP), 4)


def reduce_rows(pieces):
    return [pieces[0]] + [lax.ppermute(pieces[s], "mlp", along(-s)) for s in (1, 2, 3)]


def per_device(
    tokens, cached_states, prompt_lengths, accepted, owner_slot,
    w_query, w_key, w_value, w_gate_ret, w_out, w_gate, w_up, w_down,
):
    requests, _, key_width, value_width = cached_states.shape
    states = cached_states.reshape(requests, key_width, value_width)
    req, mlp = lax.axis_index("req"), lax.axis_index("mlp")
    z, core = mlp // 2, mlp % 2
    place = jnp.stack([req // 4, req % 4, z, core]).astype(jnp.int32)
    gamma = 1.0 - jnp.exp2(-5.0 - mlp.astype(F32))
    decay = jnp.log(gamma)
    old = jnp.exp(decay * accepted.astype(F32))

    swapped = lax.ppermute(tokens, "mlp", SWAP)
    part_a, part_b, normed = prepare(w_gate, w_up, w_down, tokens, swapped)
    xs = lax.all_to_all(
        normed, "mlp", split_axis=0, concat_axis=0, tiled=True,
        axis_index_groups=[[c, 2 + c, 4 + c, 6 + c] for c in range(2)],
    )
    block_a, block_b = join(ring(part_a, "y"), ring(part_b, "x"))
    near = [hop(block_a, "x", 1), hop(block_a, "x", -1), hop(block_b, "y", 1), hop(block_b, "y", -1)]

    ids = jnp.arange(requests, dtype=jnp.int32)
    block = ids // 2
    order = ((z - block % 4) % 4 * 2 + (core + block // 4) % 2) * 2 + ids % 2
    pick = order[:, None] == ids[None, :]
    lengths = jnp.sum(jnp.where(pick, prompt_lengths[None, :], 0), axis=1)
    kept = jnp.sum(jnp.where(pick, accepted[None, :], 0), axis=1)
    rows, half = requests * DRAFT, key_width // 2
    draft = jnp.arange(DRAFT, dtype=jnp.int32)
    position = (lengths[:, None] + draft[None, :]).astype(F32).reshape(-1)
    ahead = (kept[:, None] - 1 - draft[None, :]).astype(F32).reshape(-1)
    freq = jnp.exp(-math.log(10000.0) * jnp.arange(half, dtype=F32) / half)
    angles = position[:, None] * freq[None, :]
    fade = jnp.where(ahead >= 0, jnp.exp(decay * jnp.maximum(ahead, 0.0)), 0.0)
    grow = jnp.exp(decay * (jnp.arange(rows, dtype=jnp.int32) % DRAFT + 1).astype(F32))
    wide = (rows, half)
    table = jnp.concatenate(
        [
            jnp.cos(angles), jnp.sin(angles),
            jnp.broadcast_to(fade[:, None], wide), jnp.broadcast_to(grow[:, None], wide),
        ],
        axis=1,
    )

    spot, _ = lax.optimization_barrier((place, block_a))
    same, other, k, v = retention(
        spot, decay.reshape(1), xs, table, w_query, w_key, w_value, w_gate_ret, w_out, states
    )
    near, (same, other, k, v) = lax.optimization_barrier((near, (same, other, k, v)))
    w_all = [block_a, near[0], near[1], hop(near[0], "x", 1), block_b, near[2], near[3], hop(near[2], "y", 1)]
    sums = reduce_rows(pair_rows(same, other))
    k, sums[1] = lax.optimization_barrier((k, sums[1]))
    fresh = fresh_states(place, owner_slot, old, states, k, v)
    fresh, w_all = lax.optimization_barrier((fresh, w_all))
    landed = lax.all_to_all(fresh, "req", split_axis=0, concat_axis=0, tiled=True)
    res, hidden_in = residual_rows(tokens, sums)
    same, other = ffn(place, gather_rows(hidden_in), w_all)
    mixed = final_rows(res, reduce_rows(pair_rows(same, other)))
    return mixed, widen(landed).reshape(cached_states.shape)


def solution(mesh):
    return jax.shard_map(
        per_device,
        mesh=mesh,
        in_specs=(
            P(("req", "mlp"), None),
            P("req", "mlp", None, None),
            P("req"),
            P("req"),
            P("req"),
            P(None, "mlp"),
            P(None, "mlp"),
            P(None, "mlp"),
            P(None, "mlp"),
            P("mlp", None),
            P("req", "mlp"),
            P("req", "mlp"),
            P("mlp", "req"),
        ),
        out_specs=(P(("req", "mlp"), None), P("req", "mlp", None, None)),
        check_vma=False,
    )
```

```python
import functools
import math

import jax
import jax.numpy as jnp
from jax import lax
from jax.experimental import pallas as pl
from jax.experimental.pallas import tpu as pltpu
from jax.sharding import PartitionSpec as P

DRAFT = 16
EPS = 1e-05
BF = jnp.bfloat16
F32 = jnp.float32
VM = pl.BlockSpec(memory_space=pltpu.VMEM)
SM = pl.BlockSpec(memory_space=pltpu.SMEM)
ANY = pl.BlockSpec(memory_space=pl.ANY)
HBM = pl.BlockSpec(memory_space=pltpu.HBM)


def sds(shape, dtype):
    return jax.ShapeDtypeStruct(shape, dtype)


def cost(flops, nbytes):
    return pl.CostEstimate(flops=flops, bytes_accessed=nbytes, transcendentals=0)


def params(mib):
    return pltpu.CompilerParams(vmem_limit_bytes=mib << 20)


def norm(v):
    centred = v - jnp.mean(v, axis=-1, keepdims=True)
    variance = jnp.mean(centred * centred, axis=-1, keepdims=True)
    return centred * lax.rsqrt(variance + EPS)


def staged(body, ins, outs, name, mib=8):
    n, m = len(ins), len(outs)

    def kernel(*refs):
        bufs, sems = refs[n + m : -1], refs[-1]
        copies = [pltpu.make_async_copy(refs[i], bufs[i], sems.at[i]) for i in range(n)]
        for c in copies:
            c.start()
        for c in copies:
            c.wait()
        body(*bufs, *refs[n : n + m])

    size = sum(v.size * v.dtype.itemsize for v in list(ins) + list(outs))
    return pl.pallas_call(
        kernel, out_shape=outs, in_specs=[ANY] * n, out_specs=[VM] * m,
        scratch_shapes=[pltpu.VMEM(v.shape, v.dtype) for v in ins]
        + [pltpu.SemaphoreType.DMA((n,))],
        cost_estimate=cost(0, size), compiler_params=params(mib), name=name,
    )(*ins)


def prepare_body(g_ref, u_ref, d_ref, x_ref, y_ref, a_ref, b_ref, o_ref):
    width = g_ref.shape[1]
    half, rows = width // 2, x_ref.shape[0]
    a_ref[:, :width] = g_ref[...]
    a_ref[:, width:] = u_ref[:, :half]
    b_ref[:, :half] = u_ref[:, half:]
    b_ref[:, half:] = d_ref[...].astype(F32).T.astype(BF)
    mine = norm(x_ref[...].astype(F32)).astype(BF)
    theirs = norm(y_ref[...].astype(F32)).astype(BF)
    for i in range(4):
        o_ref[i, :rows, :] = mine
        o_ref[i, rows:, :] = theirs


def prepare(g, u, d, x, y):
    part = sds((g.shape[0], 3 * g.shape[1] // 2), BF)
    both = sds((4, 2 * x.shape[0], x.shape[1]), BF)
    return staged(prepare_body, (g, u, d, x, y), [part, part, both], "prepare", 62)


def pair_body(a_ref, b_ref, *o_refs):
    rows = o_refs[0].shape[0]
    for i, o_ref in enumerate(o_refs):
        part = pl.ds(i * rows, rows)
        o_ref[...] = (a_ref[part, :].astype(F32) + b_ref[part, :].astype(F32)).astype(BF)


def pair_sum(a, b, pieces):
    piece = sds((a.shape[0] // pieces, a.shape[1]), BF)
    return staged(pair_body, (a, b), [piece] * pieces, "pair_sum")


def total(refs):
    out = refs[0][...].astype(F32)
    for r in refs[1:]:
        out = out + r[...].astype(F32)
    return out


def residual_body(x_ref, a_ref, b_ref, c_ref, d_ref, res_ref, hid_ref):
    res = x_ref[...].astype(F32) + total((a_ref, b_ref, c_ref, d_ref))
    res_ref[...] = res
    hid_ref[...] = norm(res).astype(BF)


def residual_rows(x, parts):
    return staged(residual_body, (x, *parts), [sds(x.shape, F32), sds(x.shape, BF)], "residual_rows")


def final_body(x_ref, a_ref, b_ref, c_ref, d_ref, o_ref):
    o_ref[...] = (x_ref[...] + total((a_ref, b_ref, c_ref, d_ref))).astype(BF)


def final_rows(x, parts):
    return staged(final_body, (x, *parts), [sds(x.shape, BF)], "final_rows")[0]


def block_slot(place, request):
    z, core = request // 4, request // 2 % 2
    block = (place[3] + core) % 2 * 4 + (place[2] - z + 4) % 4
    return block * 2 + request % 2


def retention_kernel(
    place, decay, *refs, rows_in, key_width, value_width
):
    x_h, table_h, wq_h, wk_h, wv_h, wg_h, wo_h, st_h = refs[:8]
    same_ref, other_ref, k_ref, v_ref = refs[8:12]
    xbuf, tableb, wbuf, wob, stb, proj, keep, joined, sems = refs[12:]
    tile = key_width
    requests = stb.shape[0]
    rows = xbuf.shape[0]
    copies = []

    def send(src, dst):
        copy = pltpu.make_async_copy(src, dst, sems.at[len(copies)])
        copy.start()
        copies.append(copy)
        return copy

    c_x = []
    for i in range(4):
        for j in range(2):
            at = (4 * j + (place[2] - i + 4) % 4) * rows_in
            rows_at = pl.ds(pl.multiple_of(at, rows_in), rows_in)
            c_x.append(send(x_h.at[i, pl.ds(j * rows_in, rows_in), :], xbuf.at[rows_at, :]))
    c_w = [send(wk_h, wbuf.at[0])]
    c_t = send(table_h, tableb)
    c_w.append(send(wq_h, wbuf.at[1]))
    for w in (wv_h, wg_h):
        for j in range(value_width // tile):
            c_w.append(send(w.at[:, pl.ds(j * tile, tile)], wbuf.at[len(c_w)]))
    c_s = [send(st_h.at[i], stb.at[block_slot(place, i)]) for i in range(requests)]
    c_o = send(wo_h, wob)
    half = key_width // 2
    row = lax.broadcasted_iota(jnp.int32, (rows, rows), 0)
    col = lax.broadcasted_iota(jnp.int32, (rows, rows), 1)
    gap = row - col
    inside = (gap >= 0) & (row // DRAFT == col // DRAFT)
    mask = jnp.where(inside, jnp.exp(decay[0] * jnp.maximum(gap, 0).astype(F32)), 0.0)
    for c in c_x:
        c.wait()

    x = xbuf[...]

    def project(j):
        c_w[j].wait()
        return jnp.dot(x, wbuf[j], preferred_element_type=F32)

    key = project(0) * (1.0 / math.sqrt(key_width))
    c_t.wait()
    cosv, sinv = tableb[:, :half], tableb[:, half : 2 * half]

    def rotate(u):
        front, back = u[:, :half], u[:, half:]
        return jnp.concatenate(
            [front * cosv - back * sinv, front * sinv + back * cosv], axis=1
        ).astype(BF)

    rk = rotate(key)
    fade = tableb[:, 2 * half : 3 * half]
    k_ref[...] = (rk.astype(F32) * jnp.concatenate([fade, fade], axis=1)).astype(BF)
    rq = rotate(project(1))
    scores = lax.dot_general(rq, rk, (((1,), (1,)), ((), ())), preferred_element_type=F32)
    weights = (scores * mask).astype(BF)
    keep[...] = rq
    for j in range(2):
        val = project(2 + j).astype(BF)
        v_ref[:, j * tile : (j + 1) * tile] = val
        proj[:, j * tile : (j + 1) * tile] = jnp.dot(weights, val, preferred_element_type=F32)
    gates = [project(4), project(5)]
    for c in c_s:
        c.wait()
    for i in range(requests):
        part = pl.ds(i * DRAFT, DRAFT)
        carried = jnp.dot(keep[part, :], stb[i].astype(BF), preferred_element_type=F32)
        grow = tableb[part, 3 * half : 4 * half]
        proj[part, :] += carried * jnp.concatenate([grow] * (value_width // half), axis=1)
    normed = norm(proj[...])
    for j in range(2):
        g = gates[j]
        act = g / (1.0 + jnp.exp(-g))
        joined[:, j * tile : (j + 1) * tile] = (
            normed[:, j * tile : (j + 1) * tile] * act
        ).astype(BF)
    c_o.wait()
    both = joined[...]
    for j in range(wob.shape[1] // 512):
        cols = pl.ds(j * 512, 512)
        out = jnp.dot(both, wob[:, cols], preferred_element_type=F32).astype(BF)
        same_ref[:, cols] = out[: rows // 2]
        other_ref[:, cols] = out[rows // 2 :]


def retention(place, decay, xs, table, wq, wk, wv, wg, wo, states):
    rows_in, width = xs.shape[1] // 2, xs.shape[2]
    rows = rows_in * 8
    key_width, value_width = wq.shape[1], wv.shape[1]
    body = functools.partial(
        retention_kernel, rows_in=rows_in, key_width=key_width, value_width=value_width
    )
    tiles = (2 * key_width + 2 * value_width) // key_width
    return pl.pallas_call(
        body,
        out_shape=[
            sds((rows // 2, width), BF), sds((rows // 2, width), BF),
            sds((rows, key_width), BF), sds((rows, value_width), BF),
        ],
        in_specs=[SM] * 2 + [ANY] * 8,
        out_specs=[VM] * 4,
        scratch_shapes=[
            pltpu.VMEM((rows, width), BF),
            pltpu.VMEM(table.shape, F32),
            pltpu.VMEM((tiles, width, key_width), BF),
            pltpu.VMEM(wo.shape, BF),
            pltpu.VMEM(states.shape, F32),
            pltpu.VMEM((rows, value_width), F32),
            pltpu.VMEM((rows, key_width), BF),
            pltpu.VMEM((rows, value_width), BF),
            pltpu.SemaphoreType.DMA((32,)),
        ],
        compiler_params=params(62),
        cost_estimate=cost(2 * rows * width * 2048, 20 << 20),
        name="retention",
    )(place, decay, xs, table, wq, wk, wv, wg, wo, states)


def fresh_kernel(place, owner, old, st_h, k_h, v_h, o_h, stb, kb, vb, ob, in_sems, out_sems):
    n = stb.shape[0]
    copies = [
        pltpu.make_async_copy(k_h, kb, in_sems.at[n]), pltpu.make_async_copy(v_h, vb, in_sems.at[n + 1])
    ]
    loads = [pltpu.make_async_copy(st_h.at[i], stb.at[i], in_sems.at[i]) for i in range(n)]
    stores = [pltpu.make_async_copy(ob.at[i], o_h.at[owner[i] // n], out_sems.at[i]) for i in range(n)]
    for c in copies + loads:
        c.start()
    for c in copies:
        c.wait()
    keys = kb[...].astype(F32).T
    values = vb[...]
    slot = lax.broadcasted_iota(jnp.int32, keys.shape, 1) // DRAFT
    for i in range(n):
        own = jnp.where(slot == block_slot(place, i), keys, 0.0).astype(BF)
        update = jnp.dot(own, values, preferred_element_type=F32)
        loads[i].wait()
        ob[i] = (old[i] * stb[i] + update).astype(BF)
        stores[i].start()
    for c in stores:
        c.wait()


def fresh_states(place, owner, old, states, k, v):
    n = states.shape[0]
    return pl.pallas_call(
        fresh_kernel,
        in_specs=[SM] * 3 + [ANY] * 3,
        out_specs=ANY,
        out_shape=sds(states.shape, BF),
        scratch_shapes=[
            pltpu.VMEM(states.shape, F32), pltpu.VMEM(k.shape, BF), pltpu.VMEM(v.shape, BF),
            pltpu.VMEM(states.shape, BF),
            pltpu.SemaphoreType.DMA((n + 2,)), pltpu.SemaphoreType.DMA((n,)),
        ],
        compiler_params=params(62),
        cost_estimate=cost(2 * states.size * DRAFT, states.size * 6),
        name="fresh_states",
    )(place, owner, old, states, k, v)


def widen_kernel(x_h, o_h, xb, ob, in_sems, out_sems):
    n = x_h.shape[0]
    loads = [pltpu.make_async_copy(x_h.at[i], xb.at[i], in_sems.at[i]) for i in range(n)]
    stores = [pltpu.make_async_copy(ob.at[i], o_h.at[i], out_sems.at[i]) for i in range(n)]
    for c in loads:
        c.start()
    for i in range(n):
        loads[i].wait()
        ob[i] = xb[i].astype(F32)
        stores[i].start()
    for c in stores:
        c.wait()


def widen(x):
    n = x.shape[0]
    return pl.pallas_call(
        widen_kernel, in_specs=[ANY], out_specs=ANY,
        out_shape=sds(x.shape, F32),
        scratch_shapes=[
            pltpu.VMEM(x.shape, BF), pltpu.VMEM(x.shape, F32),
            pltpu.SemaphoreType.DMA((n,)), pltpu.SemaphoreType.DMA((n,)),
        ],
        compiler_params=params(62),
        cost_estimate=cost(x.size, x.size * 6), name="widen",
    )(x)


def ring_order(me):
    return [me, (me + 3) % 4, (me + 1) % 4, (me + 2) % 4]


def ffn_kernel(place, *refs, rows_in):
    xs = refs[:8]
    w_refs = refs[8:16]
    same_ref, other_ref, xbuf, wa, wb, hid, sems = refs[16:]
    copies = []

    def send(src, dst):
        copy = pltpu.make_async_copy(src, dst, sems.at[len(copies)])
        copy.start()
        copies.append(copy)
        return copy

    c_x = [send(x, xbuf.at[pl.ds(i * rows_in, rows_in), :]) for i, x in enumerate(xs)]
    shard = xbuf.shape[1] // 16
    px, py = ring_order(place[0]), ring_order(place[1])

    def spread(refs, buf, outer, inner):
        out = []
        for i in range(16):
            at = outer[i // 4], inner[i % 4]
            where = (at[0] * 4 + at[1]) if buf is wa else (at[1] * 4 + at[0])
            rows = pl.ds(pl.multiple_of(where * shard, shard), shard)
            out.append(send(refs[i // 4].at[pl.ds(i % 4 * shard, shard), :], buf.at[rows, :]))
        return out

    c_a = spread(w_refs[:4], wa, px, py)
    c_b = spread(w_refs[4:], wb, py, px)
    for c in c_x + c_a:
        c.wait()
    x = xbuf[...]

    def act(g, u):
        return (g / (1.0 + jnp.exp(-g)) * u).astype(BF)

    g0 = jnp.dot(x, wa[:, 0:256], preferred_element_type=F32)
    u0 = jnp.dot(x, wa[:, 512:768], preferred_element_type=F32)
    hid[0] = act(g0, u0)
    g1 = jnp.dot(x, wa[:, 256:512], preferred_element_type=F32)
    for c in c_b:
        c.wait()
    u1 = jnp.dot(x, wb[:, 0:256], preferred_element_type=F32)
    hid[1] = act(g1, u1)
    rows = xbuf.shape[0] // 2
    contract = (((1,), (1,)), ((), ()))
    for j in range(xbuf.shape[1] // 512):
        cols = pl.ds(j * 512, 512)
        out = lax.dot_general(hid[0], wb[cols, 256:512], contract, preferred_element_type=F32)
        out += lax.dot_general(hid[1], wb[cols, 512:768], contract, preferred_element_type=F32)
        out = out.astype(BF)
        same_ref[:, cols] = out[:rows]
        other_ref[:, cols] = out[rows:]


def ffn(place, xs, w):
    rows_in, width = xs[0].shape
    rows = rows_in * 8
    return pl.pallas_call(
        functools.partial(ffn_kernel, rows_in=rows_in),
        out_shape=[sds((rows // 2, width), BF)] * 2,
        in_specs=[SM] + [ANY] * 16,
        out_specs=[VM] * 2,
        scratch_shapes=[
            pltpu.VMEM((rows, width), BF),
            pltpu.VMEM((width, 768), BF),
            pltpu.VMEM((width, 768), BF),
            pltpu.VMEM((2, rows, 256), BF),
            pltpu.SemaphoreType.DMA((40,)),
        ],
        compiler_params=params(62),
        cost_estimate=cost(2 * rows * width * 1536, 9 << 20),
        name="feed_forward",
    )(place, *xs, *w)


def hop(v, axis, shift):
    pairs = [
        (x * 4 + y, (x + shift) % 4 * 4 + y if axis == "x" else x * 4 + (y + shift) % 4)
        for x in range(4)
        for y in range(4)
    ]
    return lax.ppermute(v, "req", pairs)


def ring(v, axis):
    before = hop(v, axis, 1)
    return [v, before, hop(v, axis, -1), hop(before, axis, 1)]


def join_kernel(*refs):
    ins, outs, sems = refs[:8], refs[8:10], refs[10]
    rows = ins[0].shape[0]
    copies = [
        pltpu.make_async_copy(r, outs[i // 4].at[pl.ds(i % 4 * rows, rows), :], sems.at[i])
        for i, r in enumerate(ins)
    ]
    for c in copies:
        c.start()
    for c in copies:
        c.wait()


def join(a, b):
    shape = sds((a[0].shape[0] * 4, a[0].shape[1]), BF)
    return pl.pallas_call(
        join_kernel, out_shape=[shape] * 2, in_specs=[ANY] * 8, out_specs=[VM] * 2,
        scratch_shapes=[pltpu.SemaphoreType.DMA((8,))],
        compiler_params=params(62), cost_estimate=cost(0, 4 << 20), name="join",
    )(*a, *b)


def along(shift):
    return [(z * 2 + c, (z + shift) % 4 * 2 + c) for z in range(4) for c in range(2)]


SWAP = [(m, m ^ 1) for m in range(8)]


def gather_rows(x):
    mine = [x] + [lax.ppermute(x, "mlp", along(s)) for s in (1, 2, 3)]
    return mine + [lax.ppermute(v, "mlp", SWAP) for v in mine]


def pair_rows(same, other):
    return pair_sum(same, lax.ppermute(other, "mlp", SWAP), 4)


def reduce_rows(pieces):
    return [pieces[0]] + [lax.ppermute(pieces[s], "mlp", along(-s)) for s in (1, 2, 3)]


def per_device(
    tokens, cached_states, prompt_lengths, accepted, owner_slot,
    w_query, w_key, w_value, w_gate_ret, w_out, w_gate, w_up, w_down,
):
    requests, _, key_width, value_width = cached_states.shape
    states = cached_states.reshape(requests, key_width, value_width)
    req, mlp = lax.axis_index("req"), lax.axis_index("mlp")
    z, core = mlp // 2, mlp % 2
    place = jnp.stack([req // 4, req % 4, z, core]).astype(jnp.int32)
    gamma = 1.0 - jnp.exp2(-5.0 - mlp.astype(F32))
    decay = jnp.log(gamma)
    old = jnp.exp(decay * accepted.astype(F32))

    swapped = lax.ppermute(tokens, "mlp", SWAP)
    part_a, part_b, normed = prepare(w_gate, w_up, w_down, tokens, swapped)
    xs = lax.all_to_all(
        normed, "mlp", split_axis=0, concat_axis=0, tiled=True,
        axis_index_groups=[[c, 2 + c, 4 + c, 6 + c] for c in range(2)],
    )

    ids = jnp.arange(requests, dtype=jnp.int32)
    block = ids // 2
    order = ((z - block % 4) % 4 * 2 + (core + block // 4) % 2) * 2 + ids % 2
    pick = order[:, None] == ids[None, :]
    lengths = jnp.sum(jnp.where(pick, prompt_lengths[None, :], 0), axis=1)
    kept = jnp.sum(jnp.where(pick, accepted[None, :], 0), axis=1)
    rows, half = requests * DRAFT, key_width // 2
    draft = jnp.arange(DRAFT, dtype=jnp.int32)
    position = (lengths[:, None] + draft[None, :]).astype(F32).reshape(-1)
    ahead = (kept[:, None] - 1 - draft[None, :]).astype(F32).reshape(-1)
    freq = jnp.exp(-math.log(10000.0) * jnp.arange(half, dtype=F32) / half)
    angles = position[:, None] * freq[None, :]
    fade = jnp.where(ahead >= 0, jnp.exp(decay * jnp.maximum(ahead, 0.0)), 0.0)
    grow = jnp.exp(decay * (jnp.arange(rows, dtype=jnp.int32) % DRAFT + 1).astype(F32))
    wide = (rows, half)
    table = jnp.concatenate(
        [
            jnp.cos(angles), jnp.sin(angles),
            jnp.broadcast_to(fade[:, None], wide), jnp.broadcast_to(grow[:, None], wide),
        ],
        axis=1,
    )

    ring_a, ring_b = ring(part_a, "y"), ring(part_b, "x")
    ring_a[0], table = lax.optimization_barrier((ring_a[0], table))
    block_a, block_b = join(ring_a, ring_b)
    near = [hop(block_a, "x", 1), hop(block_a, "x", -1), hop(block_b, "y", 1), hop(block_b, "y", -1)]

    spot, _ = lax.optimization_barrier((place, block_a))
    same, other, k, v = retention(
        spot, decay.reshape(1), xs, table, w_query, w_key, w_value, w_gate_ret, w_out, states
    )
    near[0], near[2], (same, other, k, v) = lax.optimization_barrier((near[0], near[2], (same, other, k, v)))
    w_all = [block_a, near[0], near[1], hop(near[0], "x", 1), block_b, near[2], near[3], hop(near[2], "y", 1)]
    sums = reduce_rows(pair_rows(same, other))
    k, sums[1], near[1], near[3] = lax.optimization_barrier((k, sums[1], near[1], near[3]))
    fresh = fresh_states(place, owner_slot, old, states, k, v)
    fresh, w_all = lax.optimization_barrier((fresh, w_all))
    landed = lax.all_to_all(fresh, "req", split_axis=0, concat_axis=0, tiled=True)
    res, hidden_in = residual_rows(tokens, sums)
    same, other = ffn(place, gather_rows(hidden_in), w_all)
    mixed = final_rows(res, reduce_rows(pair_rows(same, other)))
    return mixed, widen(landed).reshape(cached_states.shape)


def solution(mesh):
    return jax.shard_map(
        per_device,
        mesh=mesh,
        in_specs=(
            P(("req", "mlp"), None),
            P("req", "mlp", None, None),
            P("req"),
            P("req"),
            P("req"),
            P(None, "mlp"),
            P(None, "mlp"),
            P(None, "mlp"),
            P(None, "mlp"),
            P("mlp", None),
            P("req", "mlp"),
            P("req", "mlp"),
            P("mlp", "req"),
        ),
        out_specs=(P(("req", "mlp"), None), P("req", "mlp", None, None)),
        check_vma=False,
    )
```

```python
import functools
import math

import jax
import jax.numpy as jnp
from jax import lax
from jax.experimental import pallas as pl
from jax.experimental.pallas import tpu as pltpu
from jax.sharding import PartitionSpec as P

DRAFT = 16
EPS = 1e-05
BF = jnp.bfloat16
F32 = jnp.float32
VM = pl.BlockSpec(memory_space=pltpu.VMEM)
SM = pl.BlockSpec(memory_space=pltpu.SMEM)
ANY = pl.BlockSpec(memory_space=pl.ANY)
HBM = pl.BlockSpec(memory_space=pltpu.HBM)


def sds(shape, dtype):
    return jax.ShapeDtypeStruct(shape, dtype)


def cost(flops, nbytes):
    return pl.CostEstimate(flops=flops, bytes_accessed=nbytes, transcendentals=0)


def params(mib):
    return pltpu.CompilerParams(vmem_limit_bytes=mib << 20)


def norm(v):
    centred = v - jnp.mean(v, axis=-1, keepdims=True)
    variance = jnp.mean(centred * centred, axis=-1, keepdims=True)
    return centred * lax.rsqrt(variance + EPS)


def staged(body, ins, outs, name, mib=8):
    n, m = len(ins), len(outs)

    def kernel(*refs):
        bufs, sems = refs[n + m : -1], refs[-1]
        copies = [pltpu.make_async_copy(refs[i], bufs[i], sems.at[i]) for i in range(n)]
        for c in copies:
            c.start()
        for c in copies:
            c.wait()
        body(*bufs, *refs[n : n + m])

    size = sum(v.size * v.dtype.itemsize for v in list(ins) + list(outs))
    return pl.pallas_call(
        kernel, out_shape=outs, in_specs=[ANY] * n, out_specs=[VM] * m,
        scratch_shapes=[pltpu.VMEM(v.shape, v.dtype) for v in ins]
        + [pltpu.SemaphoreType.DMA((n,))],
        cost_estimate=cost(0, size), compiler_params=params(mib), name=name,
    )(*ins)


def prepare_body(g_ref, u_ref, d_ref, x_ref, y_ref, a_ref, b_ref, o_ref):
    width = g_ref.shape[1]
    half, rows = width // 2, x_ref.shape[0]
    a_ref[:, :width] = g_ref[...]
    a_ref[:, width:] = u_ref[:, :half]
    b_ref[:, :half] = u_ref[:, half:]
    b_ref[:, half:] = d_ref[...].astype(F32).T.astype(BF)
    mine = norm(x_ref[...].astype(F32)).astype(BF)
    theirs = norm(y_ref[...].astype(F32)).astype(BF)
    for i in range(4):
        o_ref[i, :rows, :] = mine
        o_ref[i, rows:, :] = theirs


def prepare(g, u, d, x, y):
    part = sds((g.shape[0], 3 * g.shape[1] // 2), BF)
    both = sds((4, 2 * x.shape[0], x.shape[1]), BF)
    return staged(prepare_body, (g, u, d, x, y), [part, part, both], "prepare", 62)


def pair_body(a_ref, b_ref, *o_refs):
    rows = o_refs[0].shape[0]
    for i, o_ref in enumerate(o_refs):
        part = pl.ds(i * rows, rows)
        o_ref[...] = (a_ref[part, :].astype(F32) + b_ref[part, :].astype(F32)).astype(BF)


def pair_sum(a, b, pieces):
    piece = sds((a.shape[0] // pieces, a.shape[1]), BF)
    return staged(pair_body, (a, b), [piece] * pieces, "pair_sum")


def total(refs):
    out = refs[0][...].astype(F32)
    for r in refs[1:]:
        out = out + r[...].astype(F32)
    return out


def residual_body(x_ref, a_ref, b_ref, c_ref, d_ref, res_ref, hid_ref):
    res = x_ref[...].astype(F32) + total((a_ref, b_ref, c_ref, d_ref))
    res_ref[...] = res
    hid_ref[...] = norm(res).astype(BF)


def residual_rows(x, parts):
    return staged(residual_body, (x, *parts), [sds(x.shape, F32), sds(x.shape, BF)], "residual_rows")


def final_body(x_ref, a_ref, b_ref, c_ref, d_ref, o_ref):
    o_ref[...] = (x_ref[...] + total((a_ref, b_ref, c_ref, d_ref))).astype(BF)


def final_rows(x, parts):
    return staged(final_body, (x, *parts), [sds(x.shape, BF)], "final_rows")[0]


def block_slot(place, request):
    z, core = request // 4, request // 2 % 2
    block = (place[3] + core) % 2 * 4 + (place[2] - z + 4) % 4
    return block * 2 + request % 2


def retention_kernel(
    place, decay, *refs, rows_in, key_width, value_width
):
    x_h, table_h, wq_h, wk_h, wv_h, wg_h, wo_h, st_h = refs[:8]
    same_ref, other_ref, k_ref, v_ref = refs[8:12]
    xbuf, tableb, wbuf, wob, stb, proj, keep, joined, sems = refs[12:]
    tile = key_width
    requests = stb.shape[0]
    rows = xbuf.shape[0]
    copies = []

    def send(src, dst):
        copy = pltpu.make_async_copy(src, dst, sems.at[len(copies)])
        copy.start()
        copies.append(copy)
        return copy

    c_x = []
    for i in range(4):
        for j in range(2):
            at = (4 * j + (place[2] - i + 4) % 4) * rows_in
            rows_at = pl.ds(pl.multiple_of(at, rows_in), rows_in)
            c_x.append(send(x_h.at[i, pl.ds(j * rows_in, rows_in), :], xbuf.at[rows_at, :]))
    c_w = [send(wk_h, wbuf.at[0])]
    c_t = send(table_h, tableb)
    c_w.append(send(wq_h, wbuf.at[1]))
    for w in (wv_h, wg_h):
        for j in range(value_width // tile):
            c_w.append(send(w.at[:, pl.ds(j * tile, tile)], wbuf.at[len(c_w)]))
    c_s = [send(st_h.at[i], stb.at[block_slot(place, i)]) for i in range(requests)]
    c_o = send(wo_h, wob)
    half = key_width // 2
    row = lax.broadcasted_iota(jnp.int32, (rows, rows), 0)
    col = lax.broadcasted_iota(jnp.int32, (rows, rows), 1)
    gap = row - col
    inside = (gap >= 0) & (row // DRAFT == col // DRAFT)
    mask = jnp.where(inside, jnp.exp(decay[0] * jnp.maximum(gap, 0).astype(F32)), 0.0)
    for c in c_x:
        c.wait()

    x = xbuf[...]

    def project(j):
        c_w[j].wait()
        return jnp.dot(x, wbuf[j], preferred_element_type=F32)

    key = project(0) * (1.0 / math.sqrt(key_width))
    c_t.wait()
    cosv, sinv = tableb[:, :half], tableb[:, half : 2 * half]

    def rotate(u):
        front, back = u[:, :half], u[:, half:]
        return jnp.concatenate(
            [front * cosv - back * sinv, front * sinv + back * cosv], axis=1
        ).astype(BF)

    rk = rotate(key)
    fade = tableb[:, 2 * half : 3 * half]
    k_ref[...] = (rk.astype(F32) * jnp.concatenate([fade, fade], axis=1)).astype(BF)
    rq = rotate(project(1))
    scores = lax.dot_general(rq, rk, (((1,), (1,)), ((), ())), preferred_element_type=F32)
    weights = (scores * mask).astype(BF)
    keep[...] = rq
    for j in range(2):
        val = project(2 + j).astype(BF)
        v_ref[:, j * tile : (j + 1) * tile] = val
        proj[:, j * tile : (j + 1) * tile] = jnp.dot(weights, val, preferred_element_type=F32)
    gates = [project(4), project(5)]
    for c in c_s:
        c.wait()
    for i in range(requests):
        part = pl.ds(i * DRAFT, DRAFT)
        carried = jnp.dot(keep[part, :], stb[i].astype(BF), preferred_element_type=F32)
        grow = tableb[part, 3 * half : 4 * half]
        proj[part, :] += carried * jnp.concatenate([grow] * (value_width // half), axis=1)
    normed = norm(proj[...])
    for j in range(2):
        g = gates[j]
        act = g / (1.0 + jnp.exp(-g))
        joined[:, j * tile : (j + 1) * tile] = (
            normed[:, j * tile : (j + 1) * tile] * act
        ).astype(BF)
    c_o.wait()
    both = joined[...]
    for j in range(wob.shape[1] // 512):
        cols = pl.ds(j * 512, 512)
        out = jnp.dot(both, wob[:, cols], preferred_element_type=F32).astype(BF)
        same_ref[:, cols] = out[: rows // 2]
        other_ref[:, cols] = out[rows // 2 :]


def retention(place, decay, xs, table, wq, wk, wv, wg, wo, states):
    rows_in, width = xs.shape[1] // 2, xs.shape[2]
    rows = rows_in * 8
    key_width, value_width = wq.shape[1], wv.shape[1]
    body = functools.partial(
        retention_kernel, rows_in=rows_in, key_width=key_width, value_width=value_width
    )
    tiles = (2 * key_width + 2 * value_width) // key_width
    return pl.pallas_call(
        body,
        out_shape=[
            sds((rows // 2, width), BF), sds((rows // 2, width), BF),
            sds((rows, key_width), BF), sds((rows, value_width), BF),
        ],
        in_specs=[SM] * 2 + [ANY] * 8,
        out_specs=[VM] * 4,
        scratch_shapes=[
            pltpu.VMEM((rows, width), BF),
            pltpu.VMEM(table.shape, F32),
            pltpu.VMEM((tiles, width, key_width), BF),
            pltpu.VMEM(wo.shape, BF),
            pltpu.VMEM(states.shape, F32),
            pltpu.VMEM((rows, value_width), F32),
            pltpu.VMEM((rows, key_width), BF),
            pltpu.VMEM((rows, value_width), BF),
            pltpu.SemaphoreType.DMA((32,)),
        ],
        compiler_params=params(62),
        cost_estimate=cost(2 * rows * width * 2048, 20 << 20),
        name="retention",
    )(place, decay, xs, table, wq, wk, wv, wg, wo, states)


def fresh_kernel(place, owner, old, st_h, k_h, v_h, o_h, stb, kb, vb, ob, in_sems, out_sems):
    n = stb.shape[0]
    copies = [
        pltpu.make_async_copy(k_h, kb, in_sems.at[n]), pltpu.make_async_copy(v_h, vb, in_sems.at[n + 1])
    ]
    loads = [pltpu.make_async_copy(st_h.at[i], stb.at[i], in_sems.at[i]) for i in range(n)]
    stores = [pltpu.make_async_copy(ob.at[i], o_h.at[owner[i] // n], out_sems.at[i]) for i in range(n)]
    for c in copies + loads:
        c.start()
    for c in copies:
        c.wait()
    keys = kb[...].astype(F32).T
    values = vb[...]
    slot = lax.broadcasted_iota(jnp.int32, keys.shape, 1) // DRAFT
    for i in range(n):
        own = jnp.where(slot == block_slot(place, i), keys, 0.0).astype(BF)
        update = jnp.dot(own, values, preferred_element_type=F32)
        loads[i].wait()
        ob[i] = (old[i] * stb[i] + update).astype(BF)
        stores[i].start()
    for c in stores:
        c.wait()


def fresh_states(place, owner, old, states, k, v):
    n = states.shape[0]
    return pl.pallas_call(
        fresh_kernel,
        in_specs=[SM] * 3 + [ANY] * 3,
        out_specs=ANY,
        out_shape=sds(states.shape, BF),
        scratch_shapes=[
            pltpu.VMEM(states.shape, F32), pltpu.VMEM(k.shape, BF), pltpu.VMEM(v.shape, BF),
            pltpu.VMEM(states.shape, BF),
            pltpu.SemaphoreType.DMA((n + 2,)), pltpu.SemaphoreType.DMA((n,)),
        ],
        compiler_params=params(62),
        cost_estimate=cost(2 * states.size * DRAFT, states.size * 6),
        name="fresh_states",
    )(place, owner, old, states, k, v)


def widen_kernel(x_h, o_h, xb, ob, in_sems, out_sems):
    n = x_h.shape[0]
    loads = [pltpu.make_async_copy(x_h.at[i], xb.at[i], in_sems.at[i]) for i in range(n)]
    stores = [pltpu.make_async_copy(ob.at[i], o_h.at[i], out_sems.at[i]) for i in range(n)]
    for c in loads:
        c.start()
    for i in range(n):
        loads[i].wait()
        ob[i] = xb[i].astype(F32)
        stores[i].start()
    for c in stores:
        c.wait()


def widen(x):
    shape = x.shape
    x = x.reshape(2 * shape[0], shape[1] // 2, shape[2])
    n = x.shape[0]
    return pl.pallas_call(
        widen_kernel, in_specs=[ANY], out_specs=ANY,
        out_shape=sds(x.shape, F32),
        scratch_shapes=[
            pltpu.VMEM(x.shape, BF), pltpu.VMEM(x.shape, F32),
            pltpu.SemaphoreType.DMA((n,)), pltpu.SemaphoreType.DMA((n,)),
        ],
        compiler_params=params(62),
        cost_estimate=cost(x.size, x.size * 6), name="widen",
    )(x).reshape(shape)


def ring_order(me):
    return [me, (me + 3) % 4, (me + 1) % 4, (me + 2) % 4]


def ffn_kernel(place, *refs, rows_in):
    xs = refs[:8]
    w_refs = refs[8:16]
    same_ref, other_ref, xbuf, wa, wb, hid, sems = refs[16:]
    copies = []

    def send(src, dst):
        copy = pltpu.make_async_copy(src, dst, sems.at[len(copies)])
        copy.start()
        copies.append(copy)
        return copy

    c_x = [send(x, xbuf.at[pl.ds(i * rows_in, rows_in), :]) for i, x in enumerate(xs)]
    shard = xbuf.shape[1] // 16
    px, py = ring_order(place[0]), ring_order(place[1])

    def spread(refs, buf, outer, inner):
        out = []
        for i in range(16):
            at = outer[i // 4], inner[i % 4]
            where = (at[0] * 4 + at[1]) if buf is wa else (at[1] * 4 + at[0])
            rows = pl.ds(pl.multiple_of(where * shard, shard), shard)
            out.append(send(refs[i // 4].at[pl.ds(i % 4 * shard, shard), :], buf.at[rows, :]))
        return out

    c_a = spread(w_refs[:4], wa, px, py)
    c_b = spread(w_refs[4:], wb, py, px)
    for c in c_x + c_a:
        c.wait()
    x = xbuf[...]

    def act(g, u):
        return (g / (1.0 + jnp.exp(-g)) * u).astype(BF)

    g0 = jnp.dot(x, wa[:, 0:256], preferred_element_type=F32)
    u0 = jnp.dot(x, wa[:, 512:768], preferred_element_type=F32)
    hid[0] = act(g0, u0)
    g1 = jnp.dot(x, wa[:, 256:512], preferred_element_type=F32)
    for c in c_b:
        c.wait()
    u1 = jnp.dot(x, wb[:, 0:256], preferred_element_type=F32)
    hid[1] = act(g1, u1)
    rows = xbuf.shape[0] // 2
    contract = (((1,), (1,)), ((), ()))
    for j in range(xbuf.shape[1] // 512):
        cols = pl.ds(j * 512, 512)
        out = lax.dot_general(hid[0], wb[cols, 256:512], contract, preferred_element_type=F32)
        out += lax.dot_general(hid[1], wb[cols, 512:768], contract, preferred_element_type=F32)
        out = out.astype(BF)
        same_ref[:, cols] = out[:rows]
        other_ref[:, cols] = out[rows:]


def ffn(place, xs, w):
    rows_in, width = xs[0].shape
    rows = rows_in * 8
    return pl.pallas_call(
        functools.partial(ffn_kernel, rows_in=rows_in),
        out_shape=[sds((rows // 2, width), BF)] * 2,
        in_specs=[SM] + [ANY] * 16,
        out_specs=[VM] * 2,
        scratch_shapes=[
            pltpu.VMEM((rows, width), BF),
            pltpu.VMEM((width, 768), BF),
            pltpu.VMEM((width, 768), BF),
            pltpu.VMEM((2, rows, 256), BF),
            pltpu.SemaphoreType.DMA((40,)),
        ],
        compiler_params=params(62),
        cost_estimate=cost(2 * rows * width * 1536, 9 << 20),
        name="feed_forward",
    )(place, *xs, *w)


def hop(v, axis, shift):
    pairs = [
        (x * 4 + y, (x + shift) % 4 * 4 + y if axis == "x" else x * 4 + (y + shift) % 4)
        for x in range(4)
        for y in range(4)
    ]
    return lax.ppermute(v, "req", pairs)


def ring(v, axis):
    before = hop(v, axis, 1)
    return [v, before, hop(v, axis, -1), hop(before, axis, 1)]


def join_kernel(*refs):
    ins, outs, sems = refs[:8], refs[8:10], refs[10]
    rows = ins[0].shape[0]
    copies = [
        pltpu.make_async_copy(r, outs[i // 4].at[pl.ds(i % 4 * rows, rows), :], sems.at[i])
        for i, r in enumerate(ins)
    ]
    for c in copies:
        c.start()
    for c in copies:
        c.wait()


def join(a, b):
    shape = sds((a[0].shape[0] * 4, a[0].shape[1]), BF)
    return pl.pallas_call(
        join_kernel, out_shape=[shape] * 2, in_specs=[ANY] * 8, out_specs=[VM] * 2,
        scratch_shapes=[pltpu.SemaphoreType.DMA((8,))],
        compiler_params=params(62), cost_estimate=cost(0, 4 << 20), name="join",
    )(*a, *b)


def along(shift):
    return [(z * 2 + c, (z + shift) % 4 * 2 + c) for z in range(4) for c in range(2)]


SWAP = [(m, m ^ 1) for m in range(8)]


def gather_rows(x):
    mine = [x] + [lax.ppermute(x, "mlp", along(s)) for s in (1, 2, 3)]
    return mine + [lax.ppermute(v, "mlp", SWAP) for v in mine]


def pair_rows(same, other):
    return pair_sum(same, lax.ppermute(other, "mlp", SWAP), 4)


def reduce_rows(pieces):
    return [pieces[0]] + [lax.ppermute(pieces[s], "mlp", along(-s)) for s in (1, 2, 3)]


def per_device(
    tokens, cached_states, prompt_lengths, accepted, owner_slot,
    w_query, w_key, w_value, w_gate_ret, w_out, w_gate, w_up, w_down,
):
    requests, _, key_width, value_width = cached_states.shape
    states = cached_states.reshape(requests, key_width, value_width)
    req, mlp = lax.axis_index("req"), lax.axis_index("mlp")
    z, core = mlp // 2, mlp % 2
    place = jnp.stack([req // 4, req % 4, z, core]).astype(jnp.int32)
    gamma = 1.0 - jnp.exp2(-5.0 - mlp.astype(F32))
    decay = jnp.log(gamma)
    old = jnp.exp(decay * accepted.astype(F32))

    swapped = lax.ppermute(tokens, "mlp", SWAP)
    part_a, part_b, normed = prepare(w_gate, w_up, w_down, tokens, swapped)
    xs = lax.all_to_all(
        normed, "mlp", split_axis=0, concat_axis=0, tiled=True,
        axis_index_groups=[[c, 2 + c, 4 + c, 6 + c] for c in range(2)],
    )

    ids = jnp.arange(requests, dtype=jnp.int32)
    block = ids // 2
    order = ((z - block % 4) % 4 * 2 + (core + block // 4) % 2) * 2 + ids % 2
    pick = order[:, None] == ids[None, :]
    lengths = jnp.sum(jnp.where(pick, prompt_lengths[None, :], 0), axis=1)
    kept = jnp.sum(jnp.where(pick, accepted[None, :], 0), axis=1)
    rows, half = requests * DRAFT, key_width // 2
    draft = jnp.arange(DRAFT, dtype=jnp.int32)
    position = (lengths[:, None] + draft[None, :]).astype(F32).reshape(-1)
    ahead = (kept[:, None] - 1 - draft[None, :]).astype(F32).reshape(-1)
    freq = jnp.exp(-math.log(10000.0) * jnp.arange(half, dtype=F32) / half)
    angles = position[:, None] * freq[None, :]
    fade = jnp.where(ahead >= 0, jnp.exp(decay * jnp.maximum(ahead, 0.0)), 0.0)
    grow = jnp.exp(decay * (jnp.arange(rows, dtype=jnp.int32) % DRAFT + 1).astype(F32))
    wide = (rows, half)
    table = jnp.concatenate(
        [
            jnp.cos(angles), jnp.sin(angles),
            jnp.broadcast_to(fade[:, None], wide), jnp.broadcast_to(grow[:, None], wide),
        ],
        axis=1,
    )

    ring_a, ring_b = ring(part_a, "y"), ring(part_b, "x")
    ring_a[0], table = lax.optimization_barrier((ring_a[0], table))
    block_a, block_b = join(ring_a, ring_b)
    near = [hop(block_a, "x", 1), hop(block_a, "x", -1), hop(block_b, "y", 1), hop(block_b, "y", -1)]

    spot, _ = lax.optimization_barrier((place, block_a))
    same, other, k, v = retention(
        spot, decay.reshape(1), xs, table, w_query, w_key, w_value, w_gate_ret, w_out, states
    )
    near[0], near[2], (same, other, k, v) = lax.optimization_barrier((near[0], near[2], (same, other, k, v)))
    w_all = [block_a, near[0], near[1], hop(near[0], "x", 1), block_b, near[2], near[3], hop(near[2], "y", 1)]
    sums = reduce_rows(pair_rows(same, other))
    k, sums[1], near[1], near[3] = lax.optimization_barrier((k, sums[1], near[1], near[3]))
    fresh = fresh_states(place, owner_slot, old, states, k, v)
    fresh, w_all = lax.optimization_barrier((fresh, w_all))
    landed = lax.all_to_all(fresh, "req", split_axis=0, concat_axis=0, tiled=True)
    res, hidden_in = residual_rows(tokens, sums)
    same, other = ffn(place, gather_rows(hidden_in), w_all)
    mixed = final_rows(res, reduce_rows(pair_rows(same, other)))
    return mixed, widen(landed).reshape(cached_states.shape)


def solution(mesh):
    return jax.shard_map(
        per_device,
        mesh=mesh,
        in_specs=(
            P(("req", "mlp"), None),
            P("req", "mlp", None, None),
            P("req"),
            P("req"),
            P("req"),
            P(None, "mlp"),
            P(None, "mlp"),
            P(None, "mlp"),
            P(None, "mlp"),
            P("mlp", None),
            P("req", "mlp"),
            P("req", "mlp"),
            P("mlp", "req"),
        ),
        out_specs=(P(("req", "mlp"), None), P("req", "mlp", None, None)),
        check_vma=False,
    )
```

```python
import functools
import math

import jax
import jax.numpy as jnp
from jax import lax
from jax.experimental import pallas as pl
from jax.experimental.pallas import tpu as pltpu
from jax.sharding import PartitionSpec as P

DRAFT = 16
EPS = 1e-05
BF = jnp.bfloat16
F32 = jnp.float32
VM = pl.BlockSpec(memory_space=pltpu.VMEM)
SM = pl.BlockSpec(memory_space=pltpu.SMEM)
ANY = pl.BlockSpec(memory_space=pl.ANY)
HBM = pl.BlockSpec(memory_space=pltpu.HBM)


def sds(shape, dtype):
    return jax.ShapeDtypeStruct(shape, dtype)


def cost(flops, nbytes):
    return pl.CostEstimate(flops=flops, bytes_accessed=nbytes, transcendentals=0)


def params(mib):
    return pltpu.CompilerParams(vmem_limit_bytes=mib << 20)


def norm(v):
    centred = v - jnp.mean(v, axis=-1, keepdims=True)
    variance = jnp.mean(centred * centred, axis=-1, keepdims=True)
    return centred * lax.rsqrt(variance + EPS)


def staged(body, ins, outs, name, mib=8):
    n, m = len(ins), len(outs)

    def kernel(*refs):
        bufs, sems = refs[n + m : -1], refs[-1]
        copies = [pltpu.make_async_copy(refs[i], bufs[i], sems.at[i]) for i in range(n)]
        for c in copies:
            c.start()
        for c in copies:
            c.wait()
        body(*bufs, *refs[n : n + m])

    size = sum(v.size * v.dtype.itemsize for v in list(ins) + list(outs))
    return pl.pallas_call(
        kernel, out_shape=outs, in_specs=[ANY] * n, out_specs=[VM] * m,
        scratch_shapes=[pltpu.VMEM(v.shape, v.dtype) for v in ins]
        + [pltpu.SemaphoreType.DMA((n,))],
        cost_estimate=cost(0, size), compiler_params=params(mib), name=name,
    )(*ins)


def prepare_body(g_ref, u_ref, d_ref, x_ref, y_ref, a_ref, b_ref, o_ref):
    width = g_ref.shape[1]
    half, rows = width // 2, x_ref.shape[0]
    a_ref[:, :width] = g_ref[...]
    a_ref[:, width:] = u_ref[:, :half]
    b_ref[:, :half] = u_ref[:, half:]
    b_ref[:, half:] = d_ref[...].astype(F32).T.astype(BF)
    mine = norm(x_ref[...].astype(F32)).astype(BF)
    theirs = norm(y_ref[...].astype(F32)).astype(BF)
    for i in range(4):
        o_ref[i, :rows, :] = mine
        o_ref[i, rows:, :] = theirs


def prepare(g, u, d, x, y):
    part = sds((g.shape[0], 3 * g.shape[1] // 2), BF)
    both = sds((4, 2 * x.shape[0], x.shape[1]), BF)
    return staged(prepare_body, (g, u, d, x, y), [part, part, both], "prepare", 62)


def pair_body(a_ref, b_ref, *o_refs):
    rows = o_refs[0].shape[0]
    for i, o_ref in enumerate(o_refs):
        part = pl.ds(i * rows, rows)
        o_ref[...] = (a_ref[part, :].astype(F32) + b_ref[part, :].astype(F32)).astype(BF)


def pair_sum(a, b, pieces):
    piece = sds((a.shape[0] // pieces, a.shape[1]), BF)
    return staged(pair_body, (a, b), [piece] * pieces, "pair_sum")


def total(refs):
    out = refs[0][...].astype(F32)
    for r in refs[1:]:
        out = out + r[...].astype(F32)
    return out


def residual_body(x_ref, a_ref, b_ref, c_ref, d_ref, res_ref, hid_ref):
    res = x_ref[...].astype(F32) + total((a_ref, b_ref, c_ref, d_ref))
    res_ref[...] = res
    hid_ref[...] = norm(res).astype(BF)


def residual_rows(x, parts):
    return staged(residual_body, (x, *parts), [sds(x.shape, F32), sds(x.shape, BF)], "residual_rows")


def final_body(x_ref, a_ref, b_ref, c_ref, d_ref, o_ref):
    o_ref[...] = (x_ref[...] + total((a_ref, b_ref, c_ref, d_ref))).astype(BF)


def final_rows(x, parts):
    return staged(final_body, (x, *parts), [sds(x.shape, BF)], "final_rows")[0]


def block_slot(place, request):
    z, core = request // 4, request // 2 % 2
    block = (place[3] + core) % 2 * 4 + (place[2] - z + 4) % 4
    return block * 2 + request % 2


def retention_kernel(
    place, decay, *refs, rows_in, key_width, value_width
):
    x_h, table_h, wq_h, wk_h, wv_h, wg_h, wo_h, st_h = refs[:8]
    same_ref, other_ref, k_ref, v_ref = refs[8:12]
    xbuf, tableb, wbuf, wob, stb, proj, keep, joined, sems = refs[12:]
    tile = key_width
    requests = stb.shape[0]
    rows = xbuf.shape[0]
    copies = []

    def send(src, dst):
        copy = pltpu.make_async_copy(src, dst, sems.at[len(copies)])
        copy.start()
        copies.append(copy)
        return copy

    c_x = []
    for i in range(4):
        for j in range(2):
            at = (4 * j + (place[2] - i + 4) % 4) * rows_in
            rows_at = pl.ds(pl.multiple_of(at, rows_in), rows_in)
            c_x.append(send(x_h.at[i, pl.ds(j * rows_in, rows_in), :], xbuf.at[rows_at, :]))
    c_w = [send(wk_h, wbuf.at[0])]
    c_t = send(table_h, tableb)
    c_w.append(send(wq_h, wbuf.at[1]))
    for w in (wv_h, wg_h):
        for j in range(value_width // tile):
            c_w.append(send(w.at[:, pl.ds(j * tile, tile)], wbuf.at[len(c_w)]))
    c_s = [send(st_h.at[i], stb.at[block_slot(place, i)]) for i in range(requests)]
    c_o = send(wo_h, wob)
    half = key_width // 2
    row = lax.broadcasted_iota(jnp.int32, (rows, rows), 0)
    col = lax.broadcasted_iota(jnp.int32, (rows, rows), 1)
    gap = row - col
    inside = (gap >= 0) & (row // DRAFT == col // DRAFT)
    mask = jnp.where(inside, jnp.exp(decay[0] * jnp.maximum(gap, 0).astype(F32)), 0.0)
    for c in c_x:
        c.wait()

    x = xbuf[...]

    def project(j):
        c_w[j].wait()
        return jnp.dot(x, wbuf[j], preferred_element_type=F32)

    key = project(0) * (1.0 / math.sqrt(key_width))
    c_t.wait()
    cosv, sinv = tableb[:, :half], tableb[:, half : 2 * half]

    def rotate(u):
        front, back = u[:, :half], u[:, half:]
        return jnp.concatenate(
            [front * cosv - back * sinv, front * sinv + back * cosv], axis=1
        ).astype(BF)

    rk = rotate(key)
    fade = tableb[:, 2 * half : 3 * half]
    k_ref[...] = (rk.astype(F32) * jnp.concatenate([fade, fade], axis=1)).astype(BF)
    rq = rotate(project(1))
    scores = lax.dot_general(rq, rk, (((1,), (1,)), ((), ())), preferred_element_type=F32)
    weights = (scores * mask).astype(BF)
    keep[...] = rq
    for j in range(2):
        val = project(2 + j).astype(BF)
        v_ref[:, j * tile : (j + 1) * tile] = val
        proj[:, j * tile : (j + 1) * tile] = jnp.dot(weights, val, preferred_element_type=F32)
    gates = [project(4), project(5)]
    for c in c_s:
        c.wait()
    for i in range(requests):
        part = pl.ds(i * DRAFT, DRAFT)
        carried = jnp.dot(keep[part, :], stb[i].astype(BF), preferred_element_type=F32)
        grow = tableb[part, 3 * half : 4 * half]
        proj[part, :] += carried * jnp.concatenate([grow] * (value_width // half), axis=1)
    normed = norm(proj[...])
    for j in range(2):
        g = gates[j]
        act = g / (1.0 + jnp.exp(-g))
        joined[:, j * tile : (j + 1) * tile] = (
            normed[:, j * tile : (j + 1) * tile] * act
        ).astype(BF)
    c_o.wait()
    both = joined[...]
    for j in range(wob.shape[1] // 512):
        cols = pl.ds(j * 512, 512)
        out = jnp.dot(both, wob[:, cols], preferred_element_type=F32).astype(BF)
        same_ref[:, cols] = out[: rows // 2]
        other_ref[:, cols] = out[rows // 2 :]


def retention(place, decay, xs, table, wq, wk, wv, wg, wo, states):
    rows_in, width = xs.shape[1] // 2, xs.shape[2]
    rows = rows_in * 8
    key_width, value_width = wq.shape[1], wv.shape[1]
    body = functools.partial(
        retention_kernel, rows_in=rows_in, key_width=key_width, value_width=value_width
    )
    tiles = (2 * key_width + 2 * value_width) // key_width
    return pl.pallas_call(
        body,
        out_shape=[
            sds((rows // 2, width), BF), sds((rows // 2, width), BF),
            sds((rows, key_width), BF), sds((rows, value_width), BF),
        ],
        in_specs=[SM] * 2 + [ANY] * 8,
        out_specs=[VM] * 4,
        scratch_shapes=[
            pltpu.VMEM((rows, width), BF),
            pltpu.VMEM(table.shape, F32),
            pltpu.VMEM((tiles, width, key_width), BF),
            pltpu.VMEM(wo.shape, BF),
            pltpu.VMEM(states.shape, F32),
            pltpu.VMEM((rows, value_width), F32),
            pltpu.VMEM((rows, key_width), BF),
            pltpu.VMEM((rows, value_width), BF),
            pltpu.SemaphoreType.DMA((32,)),
        ],
        compiler_params=params(62),
        cost_estimate=cost(2 * rows * width * 2048, 20 << 20),
        name="retention",
    )(place, decay, xs, table, wq, wk, wv, wg, wo, states)


def fresh_kernel(place, owner, old, st_h, k_h, v_h, o_h, stb, kb, vb, ob, in_sems, out_sems):
    n = stb.shape[0]
    copies = [
        pltpu.make_async_copy(k_h, kb, in_sems.at[n]), pltpu.make_async_copy(v_h, vb, in_sems.at[n + 1])
    ]
    loads = [pltpu.make_async_copy(st_h.at[i], stb.at[i], in_sems.at[i]) for i in range(n)]
    stores = [pltpu.make_async_copy(ob.at[i], o_h.at[owner[i] // n], out_sems.at[i]) for i in range(n)]
    for c in copies + loads:
        c.start()
    for c in copies:
        c.wait()
    keys = kb[...].astype(F32).T
    values = vb[...]
    slot = lax.broadcasted_iota(jnp.int32, keys.shape, 1) // DRAFT
    for i in range(n):
        own = jnp.where(slot == block_slot(place, i), keys, 0.0).astype(BF)
        update = jnp.dot(own, values, preferred_element_type=F32)
        loads[i].wait()
        ob[i] = (old[i] * stb[i] + update).astype(BF)
        stores[i].start()
    for c in stores:
        c.wait()


def fresh_states(place, owner, old, states, k, v):
    n = states.shape[0]
    return pl.pallas_call(
        fresh_kernel,
        in_specs=[SM] * 3 + [ANY] * 3,
        out_specs=ANY,
        out_shape=sds(states.shape, BF),
        scratch_shapes=[
            pltpu.VMEM(states.shape, F32), pltpu.VMEM(k.shape, BF), pltpu.VMEM(v.shape, BF),
            pltpu.VMEM(states.shape, BF),
            pltpu.SemaphoreType.DMA((n + 2,)), pltpu.SemaphoreType.DMA((n,)),
        ],
        compiler_params=params(62),
        cost_estimate=cost(2 * states.size * DRAFT, states.size * 6),
        name="fresh_states",
    )(place, owner, old, states, k, v)


def widen_kernel(x_h, o_h, xb, ob, in_sems, out_sems):
    n = x_h.shape[0]
    loads = [pltpu.make_async_copy(x_h.at[i], xb.at[i], in_sems.at[i]) for i in range(n)]
    stores = [pltpu.make_async_copy(ob.at[i], o_h.at[i], out_sems.at[i]) for i in range(n)]
    for c in loads:
        c.start()
    for i in range(n):
        loads[i].wait()
        ob[i] = xb[i].astype(F32)
        stores[i].start()
    for c in stores:
        c.wait()


def widen(x):
    n = x.shape[0]
    return pl.pallas_call(
        widen_kernel, in_specs=[ANY], out_specs=ANY,
        out_shape=sds(x.shape, F32),
        scratch_shapes=[
            pltpu.VMEM(x.shape, BF), pltpu.VMEM(x.shape, F32),
            pltpu.SemaphoreType.DMA((n,)), pltpu.SemaphoreType.DMA((n,)),
        ],
        compiler_params=params(62),
        cost_estimate=cost(x.size, x.size * 6), name="widen",
    )(x)


def ring_order(me):
    return [me, (me + 3) % 4, (me + 1) % 4, (me + 2) % 4]


def ffn_kernel(place, *refs, rows_in):
    xs = refs[:8]
    w_refs = refs[8:16]
    same_ref, other_ref, xbuf, wa, wb, hid, sems = refs[16:]
    copies = []

    def send(src, dst):
        copy = pltpu.make_async_copy(src, dst, sems.at[len(copies)])
        copy.start()
        copies.append(copy)
        return copy

    c_x = [send(x, xbuf.at[pl.ds(i * rows_in, rows_in), :]) for i, x in enumerate(xs)]
    shard = xbuf.shape[1] // 16
    px, py = ring_order(place[0]), ring_order(place[1])

    def spread(refs, buf, outer, inner):
        out = []
        for i in range(16):
            at = outer[i // 4], inner[i % 4]
            where = (at[0] * 4 + at[1]) if buf is wa else (at[1] * 4 + at[0])
            rows = pl.ds(pl.multiple_of(where * shard, shard), shard)
            out.append(send(refs[i // 4].at[pl.ds(i % 4 * shard, shard), :], buf.at[rows, :]))
        return out

    c_a = spread(w_refs[:4], wa, px, py)
    c_b = spread(w_refs[4:], wb, py, px)
    for c in c_x + c_a:
        c.wait()
    x = xbuf[...]

    def act(g, u):
        return (g / (1.0 + jnp.exp(-g)) * u).astype(BF)

    g0 = jnp.dot(x, wa[:, 0:256], preferred_element_type=F32)
    u0 = jnp.dot(x, wa[:, 512:768], preferred_element_type=F32)
    hid[0] = act(g0, u0)
    g1 = jnp.dot(x, wa[:, 256:512], preferred_element_type=F32)
    for c in c_b:
        c.wait()
    u1 = jnp.dot(x, wb[:, 0:256], preferred_element_type=F32)
    hid[1] = act(g1, u1)
    rows = xbuf.shape[0] // 2
    contract = (((1,), (1,)), ((), ()))
    for j in range(xbuf.shape[1] // 512):
        cols = pl.ds(j * 512, 512)
        out = lax.dot_general(hid[0], wb[cols, 256:512], contract, preferred_element_type=F32)
        out += lax.dot_general(hid[1], wb[cols, 512:768], contract, preferred_element_type=F32)
        out = out.astype(BF)
        same_ref[:, cols] = out[:rows]
        other_ref[:, cols] = out[rows:]


def ffn(place, xs, w):
    rows_in, width = xs[0].shape
    rows = rows_in * 8
    return pl.pallas_call(
        functools.partial(ffn_kernel, rows_in=rows_in),
        out_shape=[sds((rows // 2, width), BF)] * 2,
        in_specs=[SM] + [ANY] * 16,
        out_specs=[VM] * 2,
        scratch_shapes=[
            pltpu.VMEM((rows, width), BF),
            pltpu.VMEM((width, 768), BF),
            pltpu.VMEM((width, 768), BF),
            pltpu.VMEM((2, rows, 256), BF),
            pltpu.SemaphoreType.DMA((40,)),
        ],
        compiler_params=params(62),
        cost_estimate=cost(2 * rows * width * 1536, 9 << 20),
        name="feed_forward",
    )(place, *xs, *w)


def hop(v, axis, shift):
    pairs = [
        (x * 4 + y, (x + shift) % 4 * 4 + y if axis == "x" else x * 4 + (y + shift) % 4)
        for x in range(4)
        for y in range(4)
    ]
    return lax.ppermute(v, "req", pairs)


def ring(v, axis):
    before = hop(v, axis, 1)
    return [v, before, hop(v, axis, -1), hop(before, axis, 1)]


def join_kernel(*refs):
    ins, outs, sems = refs[:8], refs[8:10], refs[10]
    rows = ins[0].shape[0]
    copies = [
        pltpu.make_async_copy(r, outs[i // 4].at[pl.ds(i % 4 * rows, rows), :], sems.at[i])
        for i, r in enumerate(ins)
    ]
    for c in copies:
        c.start()
    for c in copies:
        c.wait()


def join(a, b):
    shape = sds((a[0].shape[0] * 4, a[0].shape[1]), BF)
    return pl.pallas_call(
        join_kernel, out_shape=[shape] * 2, in_specs=[ANY] * 8, out_specs=[VM] * 2,
        scratch_shapes=[pltpu.SemaphoreType.DMA((8,))],
        compiler_params=params(62), cost_estimate=cost(0, 4 << 20), name="join",
    )(*a, *b)


def along(shift):
    return [(z * 2 + c, (z + shift) % 4 * 2 + c) for z in range(4) for c in range(2)]


SWAP = [(m, m ^ 1) for m in range(8)]


def gather_rows(x):
    mine = [x] + [lax.ppermute(x, "mlp", along(s)) for s in (1, 2, 3)]
    return mine + [lax.ppermute(v, "mlp", SWAP) for v in mine]


def pair_rows(same, other):
    return pair_sum(same, lax.ppermute(other, "mlp", SWAP), 4)


def reduce_rows(pieces):
    return [pieces[0]] + [lax.ppermute(pieces[s], "mlp", along(-s)) for s in (1, 2, 3)]


def per_device(
    tokens, cached_states, prompt_lengths, accepted, owner_slot,
    w_query, w_key, w_value, w_gate_ret, w_out, w_gate, w_up, w_down,
):
    requests, _, key_width, value_width = cached_states.shape
    states = cached_states.reshape(requests, key_width, value_width)
    req, mlp = lax.axis_index("req"), lax.axis_index("mlp")
    z, core = mlp // 2, mlp % 2
    place = jnp.stack([req // 4, req % 4, z, core]).astype(jnp.int32)
    gamma = 1.0 - jnp.exp2(-5.0 - mlp.astype(F32))
    decay = jnp.log(gamma)
    old = jnp.exp(decay * accepted.astype(F32))

    swapped = lax.ppermute(tokens, "mlp", SWAP)
    part_a, part_b, normed = prepare(w_gate, w_up, w_down, tokens, swapped)
    xs = lax.all_to_all(
        normed, "mlp", split_axis=0, concat_axis=0, tiled=True,
        axis_index_groups=[[c, 2 + c, 4 + c, 6 + c] for c in range(2)],
    )

    ids = jnp.arange(requests, dtype=jnp.int32)
    block = ids // 2
    order = ((z - block % 4) % 4 * 2 + (core + block // 4) % 2) * 2 + ids % 2
    pick = order[:, None] == ids[None, :]
    lengths = jnp.sum(jnp.where(pick, prompt_lengths[None, :], 0), axis=1)
    kept = jnp.sum(jnp.where(pick, accepted[None, :], 0), axis=1)
    rows, half = requests * DRAFT, key_width // 2
    draft = jnp.arange(DRAFT, dtype=jnp.int32)
    position = (lengths[:, None] + draft[None, :]).astype(F32).reshape(-1)
    ahead = (kept[:, None] - 1 - draft[None, :]).astype(F32).reshape(-1)
    freq = jnp.exp(-math.log(10000.0) * jnp.arange(half, dtype=F32) / half)
    angles = position[:, None] * freq[None, :]
    fade = jnp.where(ahead >= 0, jnp.exp(decay * jnp.maximum(ahead, 0.0)), 0.0)
    grow = jnp.exp(decay * (jnp.arange(rows, dtype=jnp.int32) % DRAFT + 1).astype(F32))
    wide = (rows, half)
    table = jnp.concatenate(
        [
            jnp.cos(angles), jnp.sin(angles),
            jnp.broadcast_to(fade[:, None], wide), jnp.broadcast_to(grow[:, None], wide),
        ],
        axis=1,
    )

    ring_a, ring_b = ring(part_a, "y"), ring(part_b, "x")
    ring_a[0], table = lax.optimization_barrier((ring_a[0], table))
    block_a, block_b = join(ring_a, ring_b)
    near = [hop(block_a, "x", 1), hop(block_a, "x", -1), hop(block_b, "y", 1), hop(block_b, "y", -1)]

    spot, _ = lax.optimization_barrier((place, block_a))
    same, other, k, v = retention(
        spot, decay.reshape(1), xs, table, w_query, w_key, w_value, w_gate_ret, w_out, states
    )
    near[0], near[2], (same, other, k, v) = lax.optimization_barrier((near[0], near[2], (same, other, k, v)))
    w_all = [block_a, near[0], near[1], hop(near[0], "x", 1), block_b, near[2], near[3], hop(near[2], "y", 1)]
    sums = reduce_rows(pair_rows(same, other))
    k, near[1], near[3] = lax.optimization_barrier((k, near[1], near[3]))
    fresh = fresh_states(place, owner_slot, old, states, k, v)
    fresh, w_all = lax.optimization_barrier((fresh, w_all))
    landed = lax.all_to_all(fresh, "req", split_axis=0, concat_axis=0, tiled=True)
    res, hidden_in = residual_rows(tokens, sums)
    same, other = ffn(place, gather_rows(hidden_in), w_all)
    mixed = final_rows(res, reduce_rows(pair_rows(same, other)))
    return mixed, widen(landed).reshape(cached_states.shape)


def solution(mesh):
    return jax.shard_map(
        per_device,
        mesh=mesh,
        in_specs=(
            P(("req", "mlp"), None),
            P("req", "mlp", None, None),
            P("req"),
            P("req"),
            P("req"),
            P(None, "mlp"),
            P(None, "mlp"),
            P(None, "mlp"),
            P(None, "mlp"),
            P("mlp", None),
            P("req", "mlp"),
            P("req", "mlp"),
            P("mlp", "req"),
        ),
        out_specs=(P(("req", "mlp"), None), P("req", "mlp", None, None)),
        check_vma=False,
    )
```
